128 devices in a mesh: grp: 8 (over y, core), blk: 16 (over z, x).
Axes of the slice: x: 4, y: 4, z: 4, core: 2. Of those that a mesh axis runs over, the one named last changes fastest.
Arguments:
- void_fraction: float32 [256, 128, 2048], P('blk', None, 'grp'), parts along dimension 2, may hold values from 0.5 to 0.95
- slip_velocity: float32 [3, 256, 128, 2048], P(None, 'blk', None, 'grp'), parts along dimension 3, may hold values from -10.5 to 10.5
- size_class: int32 [32, 16, 256], P('blk', None, 'grp'), parts along dimension 2, may hold values from 0 to 3
- class_scale: float32 [4], replicated, may hold values from 0.5 to 2
Outputs:
- corrected_drag: float32 [3, 256, 128, 2048], P(None, 'blk', None, 'grp'), parts along dimension 3
The draws below stay inside these ranges and needn't reach their ends.
There are 8 independent parts, one for each index of `grp`. The reference program is written for one: setup_inputs(seed, part) draws one part's arguments, and reference() takes and returns one part's arrays. A program takes and returns all parts, laid end to end along the dimension named above; an argument that names none is the same for every part. Nothing has to cross between parts.
All inputs are finite; a program needn't handle non-finite values.
Results may differ from the reference program's by a relative error of at most 0.00025.
Values sent between devices are 32-bit elements; how exact they have to be, the bound alone decides.
No kernel may reach another device: no remote copies, remote signals or barrier semaphores. Data moves between devices by JAX's collectives and lax.ppermute only.
A program may use at most 128 MiB of HBM per device.

```python
import math
import jax
import jax.numpy as jnp
from jax import lax

NY = 128
NZ = 256
KCLS = 4
NX = 256


def spread_blocks(block_part):
    return jnp.repeat(jnp.repeat(jnp.repeat(block_part, 8, -3), 8, -2), 8, -1)


def draw_void_fraction(key, part):
    cell_key, block_key = jax.random.split(key)
    cell_part = jax.random.uniform(cell_key, (NX, NY, NZ), jnp.float32)
    block_part = spread_blocks(jax.random.uniform(block_key, (NX // 8, NY // 8, NZ // 8), jnp.float32))
    blended = 0.5 * cell_part + 0.5 * block_part
    return 0.5 + 0.45 * blended


def draw_slip_velocity(key, part):
    cell_key, block_key = jax.random.split(key)
    x_frac = jnp.arange(NX).astype(jnp.float32) / NX
    y_frac = (jnp.arange(NY) * 37 % NY).astype(jnp.float32) / NY
    amplitude = 0.5 * jnp.exp(0.7655 * x_frac)[:, None] * jnp.exp(0.7655 * y_frac)[None, :]
    cell_part = jax.random.truncated_normal(cell_key, -3.0, 3.0, (3, NX, NY, NZ), jnp.float32)
    block_part = spread_blocks(jax.random.truncated_normal(block_key, -3.0, 3.0, (3, NX // 8, NY // 8, NZ // 8), jnp.float32))
    field = amplitude[None, :, :, None] * (0.7 * cell_part + 0.7 * block_part)
    return field


def plant(result, rng, least, top_value):
    shape = result.shape
    spot = [jax.random.randint(jax.random.fold_in(rng, axis), (), 0, shape[axis]) for axis in range(len(shape))]
    result = result.at[tuple(spot)].set(least)
    longest = shape.index(max(shape))
    spot[longest] = (spot[longest] + 1) % shape[longest]
    return result.at[tuple(spot)].set(top_value)


def setup_inputs(seed: int = 0, part: int = 0) -> dict:
    keys = jax.random.split(jax.random.key(seed), 5)
    part_splits = jax.random.split(jax.random.fold_in(keys[4], part), 5)
    void_fraction = draw_void_fraction(jax.random.fold_in(jax.random.fold_in(keys[4], part), 71), part)
    slip_velocity = draw_slip_velocity(jax.random.fold_in(jax.random.fold_in(keys[4], part), 71), part)
    size_class = plant(jax.random.randint(part_splits[2], (NX // 8, NY // 8, NZ // 8), 0, KCLS), jax.random.fold_in(part_splits[2], 1), 0, KCLS - 1).astype(jnp.int32)
    class_scale = jnp.clip(jnp.exp(jax.random.uniform(keys[3], (KCLS,), jnp.float32, math.log(0.5), math.log(2.0))), 0.5, 2.0)
    return dict(void_fraction=void_fraction, slip_velocity=slip_velocity, size_class=size_class, class_scale=class_scale)


def axis_restrict(values, dimension, periodic):
    length = values.shape[dimension]
    coarse_len = length // 2
    even_part = lax.slice_in_dim(values, 0, length, 2, dimension)
    odd_part = lax.slice_in_dim(values, 1, length, 2, dimension)
    if periodic:
        behind = jnp.roll(odd_part, 1, dimension)
        ahead_cells = jnp.roll(even_part, -1, dimension)
    else:
        behind = jnp.concatenate([lax.slice_in_dim(even_part, 0, 1, 1, dimension), lax.slice_in_dim(odd_part, 0, coarse_len - 1, 1, dimension)], dimension)
        ahead_cells = jnp.concatenate([lax.slice_in_dim(even_part, 1, coarse_len, 1, dimension), lax.slice_in_dim(odd_part, coarse_len - 1, coarse_len, 1, dimension)], dimension)
    return (behind + 3.0 * even_part + 3.0 * odd_part + ahead_cells) * 0.125

def axis_prolong(values, dimension, periodic):
    length = values.shape[dimension]
    if periodic:
        behind = jnp.roll(values, 1, dimension)
        ahead_cells = jnp.roll(values, -1, dimension)
    else:
        behind = jnp.concatenate([lax.slice_in_dim(values, 0, 1, 1, dimension), lax.slice_in_dim(values, 0, length - 1, 1, dimension)], dimension)
        ahead_cells = jnp.concatenate([lax.slice_in_dim(values, 1, length, 1, dimension), lax.slice_in_dim(values, length - 1, length, 1, dimension)], dimension)
    lower_cells = (3.0 * values + behind) * 0.25
    upper_cells = (3.0 * values + ahead_cells) * 0.25
    new_shape = list(values.shape)
    new_shape[dimension] = 2 * length
    return jnp.stack([lower_cells, upper_cells], dimension + 1).reshape(new_shape)

def restrict_all(values):
    return axis_restrict(axis_restrict(axis_restrict(values, 1, True), 2, True), 3, False)

def prolong_all(values):
    return axis_prolong(axis_prolong(axis_prolong(values, 1, True), 2, True), 3, False)

def drag_force(void_level, slip_level, kappa_field):
    slip_speed = jnp.sqrt(lax.optimization_barrier(jnp.sum(slip_level * slip_level, axis=0)))
    factor = kappa_field * (1.0 - void_level) * jnp.exp(-1.65 * jnp.log(void_level)) * slip_speed
    return factor[None] * slip_level

def class_lookup(size_class, class_scale):
    labels = jnp.arange(class_scale.shape[0], dtype=jnp.int32)
    chosen = jnp.where(size_class[..., None] == labels, class_scale, 0.0)
    return lax.optimization_barrier(jnp.sum(chosen, axis=-1))

def expand_blocks(block_values, repeat_count):
    extent_x, extent_y, extent_z = block_values.shape
    widened = jnp.broadcast_to(block_values[:, None, :, None, :, None], (extent_x, repeat_count, extent_y, repeat_count, extent_z, repeat_count))
    return widened.reshape(extent_x * repeat_count, extent_y * repeat_count, extent_z * repeat_count)

def plane_terms(filtered, slip_level, drag_level):
    return (lax.optimization_barrier(jnp.sum(filtered * slip_level, axis=(0, 1, 2))), lax.optimization_barrier(jnp.sum(drag_level * slip_level, axis=(0, 1, 2))))

def reference(void_fraction, slip_velocity, size_class, class_scale):
    kappa_block = class_lookup(size_class, class_scale)
    void_level = void_fraction
    slip_level = slip_velocity
    drag_level = drag_force(void_level, slip_level, expand_blocks(kappa_block, 8))
    drag_levels = [drag_level]
    ratios = []
    for level_index in range(1, 4):
        stacked = jnp.concatenate([void_level[None], slip_level, drag_level], 0)
        coarse = restrict_all(stacked)
        void_level = coarse[0]
        slip_level = coarse[1:4]
        filtered = coarse[4:7]
        drag_level = drag_force(void_level, slip_level, expand_blocks(kappa_block, 8 >> level_index))
        numerator, denominator = plane_terms(filtered, slip_level, drag_level)
        ratios.append(numerator / denominator)
        drag_levels.append(drag_level)
    correction = (ratios[2] - 1.0) * drag_levels[3]
    correction = prolong_all(correction) + (ratios[1] - 1.0) * drag_levels[2]
    correction = prolong_all(correction) + (ratios[0] - 1.0) * drag_levels[1]
    return drag_levels[0] + prolong_all(correction)
```

```python
import functools

import jax
import jax.numpy as jnp
from jax import lax
from jax.experimental import pallas as pl
from jax.experimental.pallas import tpu as pltpu
from jax.sharding import PartitionSpec as P

F32 = jnp.float32
BF16 = jnp.bfloat16
ROWS = 16
NY = 128
NZ = 256
LEAD = 8


def iota(shape, axis):
    return lax.broadcasted_iota(jnp.int32, shape, axis)


def restrict_z(length, width=None, shift=0):
    width = width or length // 2
    fine = iota((length, width), 0)
    coarse = iota((length, width), 1) - shift
    offset = fine - 2 * coarse
    weight = jnp.where((offset == 0) | (offset == 1), 3.0, 0.0)
    weight = weight + jnp.where((offset == -1) | (offset == 2), 1.0, 0.0)
    weight = weight + jnp.where((fine == 0) & (coarse == 0), 1.0, 0.0)
    last = length // 2 - 1
    weight = weight + jnp.where((fine == length - 1) & (coarse == last), 1.0, 0.0)
    weight = jnp.where((coarse >= 0) & (coarse <= last), weight, 0.0)
    return (weight * (1.0 / 512.0)).astype(BF16)


def prolong_z(length):
    coarse = iota((length, 2 * length), 0)
    fine = iota((length, 2 * length), 1)
    centre = lax.shift_right_logical(fine, 1)
    neighbour = jnp.clip(centre - 1 + 2 * (fine & 1), 0, length - 1)
    weight = jnp.where(coarse == centre, 3.0, 0.0) + jnp.where(coarse == neighbour, 1.0, 0.0)
    return (weight * (1.0 / 64.0)).astype(BF16)


def spread(values, rows, lanes):
    a, b = values.shape
    along = (iota((b, lanes), 0) == iota((b, lanes), 1) // (lanes // b)).astype(BF16)
    wide = jnp.dot(values.astype(BF16), along, preferred_element_type=F32)
    if rows == a:
        return wide
    down = (iota((rows, a), 1) == iota((rows, a), 0) // (rows // a)).astype(BF16)
    return jnp.dot(down, wide.astype(BF16), preferred_element_type=F32)


def class_factor(scale_ref, classes):
    chosen = jnp.where(classes < 0.5, scale_ref[0], scale_ref[1])
    chosen = jnp.where(classes < 1.5, chosen, scale_ref[2])
    return jnp.where(classes < 2.5, chosen, scale_ref[3])


def drag(void, s0, s1, s2, kappa):
    speed = jnp.sqrt(s0 * s0 + s1 * s1 + s2 * s2)
    factor = kappa * (1.0 - void) * jnp.exp(-1.65 * jnp.log(void)) * speed
    return factor * s0, factor * s1, factor * s2


def split_store(value, hi_ref, lo_ref, start):
    hi = value.astype(BF16)
    rows = value.shape[0]
    hi_ref[pl.ds(start, rows), 0 : value.shape[1]] = hi
    lo_ref[pl.ds(start, rows), 0 : value.shape[1]] = (value - hi.astype(F32)).astype(BF16)


def dot2(hi, lo, table):
    return jnp.dot(hi, table, preferred_element_type=F32) + jnp.dot(
        lo, table, preferred_element_type=F32
    )


def wrap_rows(pad, q, rows):
    pad[q, LEAD - 1 : LEAD] = pad[q, LEAD + rows - 1 : LEAD + rows]
    pad[q, LEAD + rows : LEAD + rows + 1] = pad[q, LEAD : LEAD + 1]


def fill_pad(pad, p, part, rows, step, lanes):
    planes = -(-lanes // 128)
    for start in range(0, rows, step):
        value = part(start, step)
        rng = slice(LEAD + start, LEAD + start + step)
        if lanes < 128:
            pad[p, rng, 0:lanes] = value
        else:
            for h in range(planes):
                pad[planes * p + h, rng] = value[:, 128 * h : 128 * h + 128]
    for h in range(planes):
        wrap_rows(pad, planes * p + h, rows)


def restrict_y(pad, p, rows, hi_ref, lo_ref, out_start, lanes, step=16):
    half = rows // 2
    step = min(step, half)
    planes = -(-lanes // 128)
    width = min(lanes, 128)
    for start in range(0, half, step):
        for h in range(planes):
            at = LEAD + 2 * start
            q = planes * p + h
            outer = pad[q, pl.ds(at - 1, step, stride=2), :] + pad[q, pl.ds(at + 2, step, stride=2), :]
            inner = pad[q, pl.ds(at, step, stride=2), :] + pad[q, pl.ds(at + 1, step, stride=2), :]
            value = (outer + 3.0 * inner)[:, 0:width]
            hi = value.astype(BF16)
            rng = slice(out_start + start, out_start + start + step)
            cols = slice(128 * h, 128 * h + width)
            hi_ref[rng, cols] = hi
            lo_ref[rng, cols] = (value - hi.astype(F32)).astype(BF16)


def prolong_y(pad, p, rows, wide, q):
    step = min(rows, 32)
    for start in range(0, rows, step):
        at = LEAD + start
        centre = 3.0 * pad[p, at : at + step]
        wide[q, pl.ds(2 * start, step, stride=2), :] = centre + pad[p, at - 1 : at - 1 + step]
        wide[q, pl.ds(2 * start + 1, step, stride=2), :] = centre + pad[p, at + 1 : at + 1 + step]


def linear_kernel(void_hbm, slip_hbm, class_ref, v_ref, even_ref, odd_ref, buf, pad, hi, lo, vbuf, wbuf, pad2, pad3, sems):
    parity = lax.axis_index("blk") % 2
    pairs = ROWS // 2

    def copies(k):
        rows = pl.ds(2 * k, 2)
        return (
            pltpu.make_async_copy(void_hbm.at[rows], buf.at[0, pl.ds(2 * k + 1, 2)], sems.at[k, 0]),
            pltpu.make_async_copy(slip_hbm.at[:, rows], buf.at[pl.ds(1, 3), pl.ds(2 * k + 1, 2)], sems.at[k, 1]),
        )

    for k in range(pairs):
        for copy in copies(k):
            copy.start()
    for c in range(4):
        for row in (0, ROWS + 1):
            for start in range(0, NY, 32):
                buf[c, row, start : start + 32] = jnp.zeros((32, NZ), F32)
    table = restrict_z(NZ)
    table_lo = restrict_z(128, 128, 0)
    table_hi = restrict_z(128, 128, 64)
    table3 = [restrict_z(64, 128, 32 * c) for c in range(4)]

    for copy in copies(0):
        copy.wait()

    def body(i, carry):
        @pl.when(i + 1 < pairs)
        def _():
            for copy in copies(i + 1):
                copy.wait()

        base = 2 * i
        for c in range(4):

            def part(start, step):
                rows = pl.ds(start, step)
                return (buf[c, base, rows] + buf[c, base + 3, rows]) + 3.0 * (
                    buf[c, base + 1, rows] + buf[c, base + 2, rows]
                )

            fill_pad(pad, c, part, NY, 32, NZ)
            restrict_y(pad, c, NY, hi, lo, c * 64, NZ)
        out = dot2(hi[...], lo[...], table)
        for c in range(4):
            v_ref[c, i] = out[c * 64 : c * 64 + 64]
            vbuf[c, i] = out[c * 64 : c * 64 + 64]
        return carry

    lax.fori_loop(0, pairs, body, 0)

    def side(ref, last):
        def row(k):
            return jnp.where(last == 1, ROWS - k, k + 1)

        def vrow(k):
            return jnp.where(last == 1, 7 - k, k)

        r0, r1, r2 = row(0), row(1), row(2)
        for group in range(2):
            for c in range(4):

                def part(start, step):
                    rows = pl.ds(start, step)
                    if group == 0:
                        return buf[c, r0, rows]
                    return 3.0 * (buf[c, r0, rows] + buf[c, r1, rows]) + buf[c, r2, rows]

                fill_pad(pad, c, part, NY, 32, NZ)
                restrict_y(pad, c, NY, hi, lo, c * 64, NZ)
            out = dot2(hi[...], lo[...], table)
            ref[256 * group : 256 * group + 256] = out
        n1, n2 = vrow(1), vrow(2)
        for c in range(4):
            fill_pad(pad2, c, lambda s, t: 3.0 * vbuf[c, n1, pl.ds(s, t)] + vbuf[c, n2, pl.ds(s, t)], 64, 32, 128)
            restrict_y(pad2, c, 64, hi, lo, c * 32, 128)
        for half in range(2):
            at = 64 * half
            ref[512 + 32 * half : 544 + 32 * half] = dot2(
                hi[at : at + 32, 0:128], lo[at : at + 32, 0:128], table_lo
            ) + dot2(hi[at + 32 : at + 64, 0:128], lo[at + 32 : at + 64, 0:128], table_hi)
        m1 = jnp.where(last == 1, 1, 0)
        m2 = jnp.where(last == 1, 0, 1)
        for c in range(4):
            fill_pad(pad3, c, lambda s, t: 3.0 * wbuf[c, m1, pl.ds(s, t)] + wbuf[c, m2, pl.ds(s, t)], 32, 32, 64)
            restrict_y(pad3, c, 32, hi, lo, c * 16, 64)
        total = jnp.zeros((16, 128), F32)
        for c in range(4):
            total = total + dot2(hi[16 * c : 16 * c + 16, 0:64], lo[16 * c : 16 * c + 16, 0:64], table3[c])
        ref[576:592] = total
        classes = jnp.where(last == 1, class_ref[1], class_ref[0]).astype(F32)
        ref[592:608] = jnp.concatenate([classes, jnp.zeros((16, 96), F32)], axis=1)

    table2 = restrict_z(128)
    for m in range(2):
        for c in range(4):
            fill_pad(
                pad2,
                c,
                lambda s, t: (vbuf[c, 2 * m + 1, pl.ds(s, t)] + vbuf[c, 2 * m + 4, pl.ds(s, t)])
                + 3.0 * (vbuf[c, 2 * m + 2, pl.ds(s, t)] + vbuf[c, 2 * m + 3, pl.ds(s, t)]),
                64,
                32,
                128,
            )
            restrict_y(pad2, c, 64, hi, lo, c * 32, 128)
        out = dot2(hi[0:128, 0:128], lo[0:128, 0:128], table2)
        for c in range(4):
            wbuf[c, m] = out[32 * c : 32 * c + 32]
    side(even_ref, 1 - parity)
    side(odd_ref, parity)


def linear_call(void, slip, classes):
    any_spec = pl.BlockSpec(memory_space=pl.ANY)
    vmem = pl.BlockSpec(memory_space=pltpu.VMEM)
    return pl.pallas_call(
        linear_kernel,
        out_shape=(
            jax.ShapeDtypeStruct((4, 8, 64, 128), F32),
            jax.ShapeDtypeStruct((608, 128), F32),
            jax.ShapeDtypeStruct((608, 128), F32),
        ),
        in_specs=[any_spec, any_spec, vmem],
        out_specs=(vmem, vmem, vmem),
        scratch_shapes=[
            pltpu.VMEM((4, ROWS + 2, NY, NZ), F32),
            pltpu.VMEM((8, NY + 16, 128), F32),
            pltpu.VMEM((256, NZ), BF16),
            pltpu.VMEM((256, NZ), BF16),
            pltpu.VMEM((4, 8, 64, 128), F32),
            pltpu.VMEM((4, 2, 32, 64), F32),
            pltpu.VMEM((4, 64 + 16, 128), F32),
            pltpu.VMEM((4, 32 + 16, 128), F32),
            pltpu.SemaphoreType.DMA((8, 2)),
        ],
        compiler_params=pltpu.CompilerParams(vmem_limit_bytes=20 << 20),
        name="linear_part",
    )(void, slip, classes)


def drag_kernel(void_hbm, slip_hbm, class_ref, scale_ref, g_hbm, filt_ref, edge_ref, buf, gbuf, kappa, pad, hi, lo, sems, out_sems):
    pairs = ROWS // 2

    def copies(k):
        rows = pl.ds(2 * k, 2)
        return (
            pltpu.make_async_copy(void_hbm.at[rows], buf.at[0, rows], sems.at[k, 0]),
            pltpu.make_async_copy(slip_hbm.at[:, rows], buf.at[pl.ds(1, 3), rows], sems.at[k, 1]),
        )

    def out_copy(k):
        return pltpu.make_async_copy(gbuf.at[:, pl.ds(2 * k + 1, 2)], g_hbm.at[:, pl.ds(2 * k, 2)], out_sems.at[k])

    for k in range(pairs):
        for copy in copies(k):
            copy.start()
    for c in range(3):
        for row in (0, ROWS + 1):
            for start in range(0, NY, 32):
                gbuf[c, row, start : start + 32] = jnp.zeros((32, NZ), F32)
    for b in range(2):
        kappa[b] = class_factor(scale_ref, spread(class_ref[b].astype(F32), 16, NZ))
    table = restrict_z(NZ)

    def drag_rows(k):
        for copy in copies(k):
            copy.wait()
        block = k // 4
        for row in range(2):
            x = 2 * k + row
            for y in range(16):
                rows = slice(8 * y, 8 * y + 8)
                factor = jnp.broadcast_to(kappa[block, y : y + 1, :], (8, NZ))
                g = drag(buf[0, x, rows], buf[1, x, rows], buf[2, x, rows], buf[3, x, rows], factor)
                for c in range(3):
                    gbuf[c, x + 1, rows] = g[c]
        out_copy(k).start()

    drag_rows(0)

    def body(i, carry):
        @pl.when(i + 1 < pairs)
        def _():
            drag_rows(i + 1)

        base = 2 * i
        for c in range(3):

            def part(start, step):
                rows = pl.ds(start, step)
                return (gbuf[c, base, rows] + gbuf[c, base + 3, rows]) + 3.0 * (
                    gbuf[c, base + 1, rows] + gbuf[c, base + 2, rows]
                )

            fill_pad(pad, c, part, NY, 32, NZ)
            restrict_y(pad, c, NY, hi, lo, c * 64, NZ)
        out = dot2(hi[...], lo[...], table)
        for c in range(3):
            filt_ref[c, i] = out[c * 64 : c * 64 + 64]
        return carry

    lax.fori_loop(0, pairs, body, 0)
    for e, row in enumerate((1, ROWS)):
        for c in range(3):
            fill_pad(pad, c, lambda s, t: gbuf[c, row, pl.ds(s, t)], NY, 32, NZ)
            restrict_y(pad, c, NY, hi, lo, c * 64, NZ)
        out = dot2(hi[...], lo[...], table)
        for c in range(3):
            edge_ref[e, c] = out[c * 64 : c * 64 + 64]
    for k in range(pairs):
        out_copy(k).wait()


def drag_call(void, slip, classes, scale):
    any_spec = pl.BlockSpec(memory_space=pl.ANY)
    vmem = pl.BlockSpec(memory_space=pltpu.VMEM)
    return pl.pallas_call(
        drag_kernel,
        out_shape=(
            jax.ShapeDtypeStruct((3, ROWS, NY, NZ), F32),
            jax.ShapeDtypeStruct((3, 8, 64, 128), F32),
            jax.ShapeDtypeStruct((2, 3, 64, 128), F32),
        ),
        in_specs=[any_spec, any_spec, vmem, pl.BlockSpec(memory_space=pltpu.SMEM)],
        out_specs=(any_spec, vmem, vmem),
        scratch_shapes=[
            pltpu.VMEM((4, ROWS, NY, NZ), F32),
            pltpu.VMEM((3, ROWS + 2, NY, NZ), F32),
            pltpu.VMEM((2, 16, NZ), F32),
            pltpu.VMEM((6, NY + 16, 128), F32),
            pltpu.VMEM((192, NZ), BF16),
            pltpu.VMEM((192, NZ), BF16),
            pltpu.SemaphoreType.DMA((8, 2)),
            pltpu.SemaphoreType.DMA((8,)),
        ],
        compiler_params=pltpu.CompilerParams(vmem_limit_bytes=24 << 20),
        cost_estimate=pl.CostEstimate(flops=60_000_000, bytes_accessed=16_000_000, transcendentals=1_500_000),
        name="drag_part",
    )(void, slip, classes, scale)


def levels_kernel(
    v_in, even_own, odd_own, even_in, odd_in, filt_ref, edge_ref, class_ref, scale_ref,
    g1_ref, g2_ref, g3_ref, sums_ref,
    v, w, z, gpad, pad, hi, lo, kap,
):
    parity = lax.axis_index("blk") % 2
    is_even = parity == 0

    def left(rows):
        return jnp.where(is_even, odd_in[rows], even_in[rows])

    def right(rows):
        return jnp.where(is_even, even_in[rows], odd_in[rows])

    def own_first(rows):
        return jnp.where(is_even, odd_own[rows], even_own[rows])

    def own_last(rows):
        return jnp.where(is_even, even_own[rows], odd_own[rows])

    for c in range(4):
        outer = slice(64 * c, 64 * c + 64)
        combined = slice(256 + 64 * c, 256 + 64 * c + 64)
        v[c, 0] = left(combined) + own_first(outer)
        v[c, 1] = v_in[c, 0] + left(outer)
        for i in range(1, 7):
            v[c, i + 1] = v_in[c, i]
        v[c, 8] = v_in[c, 7] + right(outer)
        v[c, 9] = right(combined) + own_last(outer)
    blocks = [
        left(slice(592, 608))[:, 0:32],
        class_ref[0].astype(F32),
        class_ref[1].astype(F32),
        right(slice(592, 608))[:, 0:32],
    ]
    for b in range(4):
        kap[b] = class_factor(scale_ref, spread(blocks[b], 64, 128))
    numerator = jnp.zeros((64, 128), F32)
    denominator = jnp.zeros((64, 128), F32)
    for i in range(10):
        slips = v[1, i], v[2, i], v[3, i]
        g = drag(v[0, i], *slips, kap[(i + 3) // 4])
        for c in range(3):
            g1_ref[c, i] = g[c]
            if i == 0:
                numerator += edge_ref[0, c] * slips[c]
            elif i == 9:
                numerator += edge_ref[1, c] * slips[c]
            else:
                numerator += filt_ref[c, i - 1] * slips[c]
                denominator += g[c] * slips[c]
    sums = [jnp.sum(numerator, axis=0, keepdims=True), jnp.sum(denominator, axis=0, keepdims=True)]

    table2 = restrict_z(128)

    def x_part(src, c, i, count):
        def part(start, step):
            rows = pl.ds(start, step)
            if i == -1:
                return 3.0 * src[c, 0, rows] + src[c, 1, rows]
            if i == count:
                return src[c, 2 * count, rows] + 3.0 * src[c, 2 * count + 1, rows]
            return (src[c, 2 * i, rows] + src[c, 2 * i + 3, rows]) + 3.0 * (
                src[c, 2 * i + 1, rows] + src[c, 2 * i + 2, rows]
            )

        return part

    n = 0
    for i in range(-1, 5):
        for c in range(4):
            fill_pad(pad, n, x_part(v, c, i, 4), 64, 32, 128)
            restrict_y(pad, n, 64, hi, lo, 32 * n, 128)
            n += 1
    for i in range(4):
        for c in range(3):
            fill_pad(pad, n, x_part(g1_ref, c, i, 4), 64, 32, 128)
            restrict_y(pad, n, 64, hi, lo, 32 * n, 128)
            n += 1
    out = dot2(hi[0 : 32 * n, 0:128], lo[0 : 32 * n, 0:128], table2)
    for i in range(6):
        for c in range(4):
            value = out[32 * (4 * i + c) : 32 * (4 * i + c) + 32]
            if i == 0 or i == 5:
                rows = slice(512 + 32 * (c // 2), 544 + 32 * (c // 2))
                beyond = left(rows) if i == 0 else right(rows)
                if c % 2:
                    beyond = pltpu.roll(beyond, 64, 1)
                value = value + beyond[:, 0:64]
            w[c, i] = value
    numerator = jnp.zeros((32, 64), F32)
    denominator = jnp.zeros((32, 64), F32)
    factors = [class_factor(scale_ref, spread(block, 32, 64)) for block in blocks]
    for i in range(6):
        slips = w[1, i], w[2, i], w[3, i]
        g = drag(w[0, i], *slips, factors[(i + 1) // 2])
        for c in range(3):
            g2_ref[c, i] = g[c]
            if 1 <= i <= 4:
                at = 32 * (24 + 3 * (i - 1) + c)
                numerator += out[at : at + 32] * slips[c]
                denominator += g[c] * slips[c]
    sums += [jnp.sum(numerator, axis=0, keepdims=True), jnp.sum(denominator, axis=0, keepdims=True)]

    table3 = restrict_z(64)
    n = 0
    for i in range(-1, 3):
        for c in range(4):
            fill_pad(gpad, n, x_part(w, c, i, 2), 32, 32, 64)
            restrict_y(gpad, n, 32, hi, lo, 16 * n, 64)
            n += 1
    for i in range(2):
        for c in range(3):
            fill_pad(gpad, n, x_part(g2_ref, c, i, 2), 32, 32, 64)
            restrict_y(gpad, n, 32, hi, lo, 16 * n, 64)
            n += 1
    out = dot2(hi[0 : 16 * n, 0:64], lo[0 : 16 * n, 0:64], table3)
    numerator = jnp.zeros((16, 32), F32)
    denominator = jnp.zeros((16, 32), F32)
    for i in range(4):
        channels = []
        for c in range(4):
            value = out[16 * (4 * i + c) : 16 * (4 * i + c) + 16]
            if i == 0 or i == 3:
                beyond = left(slice(576, 592)) if i == 0 else right(slice(576, 592))
                if c:
                    beyond = pltpu.roll(beyond, 128 - 32 * c, 1)
                value = value + beyond[:, 0:32]
            channels.append(value)
        g = drag(*channels, class_factor(scale_ref, blocks[i]))
        for c in range(3):
            g3_ref[c, i] = g[c]
            if 1 <= i <= 2:
                at = 16 * (16 + 3 * (i - 1) + c)
                numerator += out[at : at + 16] * channels[c + 1]
                denominator += g[c] * channels[c + 1]
    sums += [jnp.sum(numerator, axis=0, keepdims=True), jnp.sum(denominator, axis=0, keepdims=True)]
    wide = [
        part if part.shape[1] == 128 else jnp.concatenate([part, jnp.zeros((1, 128 - part.shape[1]), F32)], axis=1)
        for part in sums
    ]
    tile = jnp.concatenate(wide + [jnp.zeros((2, 128), F32)], axis=0)
    for d in range(16):
        sums_ref[d] = tile


def levels_call(v_part, even_own, odd_own, even_in, odd_in, filt, edge, classes, scale):
    vmem = pl.BlockSpec(memory_space=pltpu.VMEM)
    return pl.pallas_call(
        levels_kernel,
        out_shape=(
            jax.ShapeDtypeStruct((3, 10, 64, 128), F32),
            jax.ShapeDtypeStruct((3, 6, 32, 64), F32),
            jax.ShapeDtypeStruct((3, 4, 16, 32), F32),
            jax.ShapeDtypeStruct((16, 8, 128), F32),
        ),
        in_specs=[vmem] * 8 + [pl.BlockSpec(memory_space=pltpu.SMEM)],
        out_specs=(vmem,) * 4,
        scratch_shapes=[
            pltpu.VMEM((4, 10, 64, 128), F32),
            pltpu.VMEM((4, 6, 32, 64), F32),
            pltpu.VMEM((4, 4, 16, 32), F32),
            pltpu.VMEM((22, 32 + 16, 128), F32),
            pltpu.VMEM((36, 64 + 16, 128), F32),
            pltpu.VMEM((36 * 32, 128), BF16),
            pltpu.VMEM((36 * 32, 128), BF16),
            pltpu.VMEM((4, 64, 128), F32),
        ],
        compiler_params=pltpu.CompilerParams(vmem_limit_bytes=16 << 20),
        name="small_levels",
    )(v_part, even_own, odd_own, even_in, odd_in, filt, edge, classes, scale)


def final_kernel(sums_ref, g1_ref, g2_ref, g3_ref, g0_ref, out_ref, c1, wide3, wide2, pad3, pad2, pad1, wide1, hi, lo, fine, table):
    step = pl.program_id(0)

    def prolong_rows(count, scaled, rows, lanes, pad, wide, z_table):
        for p in range(count):
            pad[p, LEAD : LEAD + rows, 0:lanes] = scaled(p)
            wrap_rows(pad, p, rows)
            prolong_y(pad, p, rows, wide, p)
            split_store(wide[p][:, 0:lanes], hi, lo, 2 * rows * p)
        total = 2 * rows * count
        return dot2(hi[0:total, 0:lanes], lo[0:total, 0:lanes], z_table)

    def make_fine(e):
        values = prolong_rows(3, lambda c: c1[c, e], 64, 128, pad1, wide1, table[...])
        for c in range(3):
            fine[e % 4, c] = values[128 * c : 128 * c + 128]

    @pl.when(step == 0)
    def _():
        table[...] = prolong_z(128)
        total = jnp.sum(sums_ref[...], axis=0)
        r1 = total[0:1] / total[1:2] - 1.0
        r2 = total[2:3, 0:64] / total[3:4, 0:64] - 1.0
        r3 = total[4:5, 0:32] / total[5:6, 0:32] - 1.0

        def x_prolong(planes, count, rows, c):
            for f in range(-1, 2 * count + 1):
                centre = (f >> 1) + 1
                beside = centre + (1 if f & 1 else -1)
                yield f + 1, 3.0 * planes(c, centre) + planes(c, beside)

        up = prolong_rows(12, lambda p: r3 * g3_ref[p // 4, p % 4], 16, 32, pad3, wide3, prolong_z(32))
        c2 = {}
        for c in range(3):
            for f, value in x_prolong(lambda c, e: up[32 * (4 * c + e) : 32 * (4 * c + e) + 32], 2, 32, c):
                c2[c, f] = value + r2 * g2_ref[c, f]
        up2 = prolong_rows(18, lambda p: c2[p // 6, p % 6], 32, 64, pad2, wide2, prolong_z(64))
        for c in range(3):
            for f, value in x_prolong(lambda c, e: up2[64 * (6 * c + e) : 64 * (6 * c + e) + 64], 4, 64, c):
                c1[c, f] = value + r1 * g1_ref[c, f]
        make_fine(0)
        make_fine(1)

    make_fine(step + 2)
    behind, here, ahead = step % 4, (step + 1) % 4, (step + 2) % 4
    for c in range(3):
        for start in range(0, NY, 16):
            rows = slice(start, start + 16)
            centre = 3.0 * fine[here, c, rows]
            out_ref[c, 0, rows] = g0_ref[c, 0, rows] + (centre + fine[behind, c, rows])
            out_ref[c, 1, rows] = g0_ref[c, 1, rows] + (centre + fine[ahead, c, rows])


def final_call(sums, g1, g2, g3, g0):
    def whole(shape):
        return pl.BlockSpec(shape, lambda i: (0,) * len(shape))

    rows = pl.BlockSpec((3, 2, NY, NZ), lambda i: (0, i, 0, 0))
    return pl.pallas_call(
        final_kernel,
        grid=(8,),
        out_shape=jax.ShapeDtypeStruct((3, ROWS, NY, NZ), F32),
        in_specs=[whole((16, 8, 128)), whole((3, 10, 64, 128)), whole((3, 6, 32, 64)), whole((3, 4, 16, 32)), rows],
        out_specs=rows,
        scratch_shapes=[
            pltpu.VMEM((3, 10, 64, 128), F32),
            pltpu.VMEM((12, 32, 128), F32),
            pltpu.VMEM((18, 64, 128), F32),
            pltpu.VMEM((12, 16 + 16, 128), F32),
            pltpu.VMEM((18, 32 + 16, 128), F32),
            pltpu.VMEM((3, 64 + 16, 128), F32),
            pltpu.VMEM((3, 128, 128), F32),
            pltpu.VMEM((18 * 64, 128), BF16),
            pltpu.VMEM((18 * 64, 128), BF16),
            pltpu.VMEM((4, 3, NY, NZ), F32),
            pltpu.VMEM((128, 256), BF16),
        ],
        compiler_params=pltpu.CompilerParams(vmem_limit_bytes=20 << 20),
        name="final_part",
    )(sums, g1, g2, g3, g0)


def shards(void_fraction, slip_velocity, size_class, class_scale):
    count = lax.axis_size("blk")
    even_pairs = [(i, i ^ 1) for i in range(count)]
    odd_pairs = [(i, (i + 1) % count if i % 2 else (i - 1) % count) for i in range(count)]
    v_part, even_own, odd_own = linear_call(void_fraction, slip_velocity, size_class)
    even_in = lax.ppermute(even_own, "blk", even_pairs)
    odd_in = lax.ppermute(odd_own, "blk", odd_pairs)
    g0, filt, edge = drag_call(void_fraction, slip_velocity, size_class, class_scale)
    g1, g2, g3, sums = levels_call(
        v_part, even_own, odd_own, even_in, odd_in, filt, edge, size_class, class_scale
    )
    sums = lax.all_to_all(sums, "blk", 0, 0)
    return final_call(sums, g1, g2, g3, g0)


def solution(mesh):
    return jax.shard_map(
        shards,
        mesh=mesh,
        in_specs=(P("blk", None, "grp"), P(None, "blk", None, "grp"), P("blk", None, "grp"), P()),
        out_specs=P(None, "blk", None, "grp"),
        check_vma=False,
    )
```

```python
import math

import jax
import jax.numpy as jnp
from jax import lax
from jax.experimental import pallas as pl
from jax.experimental.pallas import tpu as pltpu
from jax.sharding import PartitionSpec as P

F32 = jnp.float32
BF16 = jnp.bfloat16
ROWS = 16
NY = 128
NZ = 256
LEAD = 8
TINY = 1.1754944e-38
POWER = -1.65 * math.log2(math.e)


def iota(shape, axis):
    return lax.broadcasted_iota(jnp.int32, shape, axis)


def restrict_z(length, width=None, shift=0):
    width = width or length // 2
    fine = iota((length, width), 0)
    coarse = iota((length, width), 1) - shift
    offset = fine - 2 * coarse
    weight = jnp.where((offset == 0) | (offset == 1), 3.0, 0.0)
    weight = weight + jnp.where((offset == -1) | (offset == 2), 1.0, 0.0)
    weight = weight + jnp.where((fine == 0) & (coarse == 0), 1.0, 0.0)
    last = length // 2 - 1
    weight = weight + jnp.where((fine == length - 1) & (coarse == last), 1.0, 0.0)
    weight = jnp.where((coarse >= 0) & (coarse <= last), weight, 0.0)
    return (weight * (1.0 / 512.0)).astype(BF16)


def spread(values, rows, lanes):
    a, b = values.shape
    along = (iota((b, lanes), 0) == iota((b, lanes), 1) // (lanes // b)).astype(BF16)
    wide = jnp.dot(values.astype(BF16), along, preferred_element_type=F32)
    if rows == a:
        return wide
    down = (iota((rows, a), 1) == iota((rows, a), 0) // (rows // a)).astype(BF16)
    return jnp.dot(down, wide.astype(BF16), preferred_element_type=F32)


def class_factor(scale_ref, classes):
    chosen = jnp.where(classes < 0.5, scale_ref[0], scale_ref[1])
    chosen = jnp.where(classes < 1.5, chosen, scale_ref[2])
    return jnp.where(classes < 2.5, chosen, scale_ref[3])


def drag(void, s0, s1, s2, kappa):
    square = s0 * s0 + s1 * s1 + s2 * s2
    speed = square * lax.rsqrt(jnp.maximum(square, TINY))
    factor = (kappa * (1.0 - void)) * (jnp.exp2(POWER * jnp.log(void)) * speed)
    return factor * s0, factor * s1, factor * s2


def dot2(hi, lo, table):
    return jnp.dot(hi, table, preferred_element_type=F32) + jnp.dot(
        lo, table, preferred_element_type=F32
    )


def wrap_rows(pad, q, rows):
    pad[q, LEAD - 1 : LEAD] = pad[q, LEAD + rows - 1 : LEAD + rows]
    pad[q, LEAD + rows : LEAD + rows + 1] = pad[q, LEAD : LEAD + 1]


def fill_pad(pad, p, part, rows, step, lanes):
    planes = -(-lanes // 128)
    for start in range(0, rows, step):
        value = part(start, step)
        rng = slice(LEAD + start, LEAD + start + step)
        if lanes < 128:
            pad[p, rng, 0:lanes] = value
        else:
            for h in range(planes):
                pad[planes * p + h, rng] = value[:, 128 * h : 128 * h + 128]
    for h in range(planes):
        wrap_rows(pad, planes * p + h, rows)


def restrict_y(pad, p, rows, hi_ref, lo_ref, out_start, lanes, step=16):
    half = rows // 2
    step = min(step, half)
    planes = -(-lanes // 128)
    width = min(lanes, 128)
    for start in range(0, half, step):
        for h in range(planes):
            at = LEAD + 2 * start
            q = planes * p + h
            outer = pad[q, pl.ds(at - 1, step, stride=2), :] + pad[q, pl.ds(at + 2, step, stride=2), :]
            inner = pad[q, pl.ds(at, step, stride=2), :] + pad[q, pl.ds(at + 1, step, stride=2), :]
            value = (outer + 3.0 * inner)[:, 0:width]
            hi = value.astype(BF16)
            rng = slice(out_start + start, out_start + start + step)
            cols = slice(128 * h, 128 * h + width)
            hi_ref[rng, cols] = hi
            lo_ref[rng, cols] = (value - hi.astype(F32)).astype(BF16)


def prolong_y(pad, p, rows, wide, q):
    step = min(rows, 32)
    for start in range(0, rows, step):
        at = LEAD + start
        centre = 3.0 * pad[p, at : at + step]
        wide[q, pl.ds(2 * start, step, stride=2), :] = centre + pad[p, at - 1 : at - 1 + step]
        wide[q, pl.ds(2 * start + 1, step, stride=2), :] = centre + pad[p, at + 1 : at + 1 + step]


def y_rows(src, lead, dst, half_rows):
    for start in range(0, half_rows, 16):
        for h in range(2):
            at = lead + 2 * start
            plane = src(h)
            outer = plane[pl.ds(at - 1, 16, stride=2), :] + plane[pl.ds(at + 2, 16, stride=2), :]
            inner = plane[pl.ds(at, 16, stride=2), :] + plane[pl.ds(at + 1, 16, stride=2), :]
            dst(h, start, outer + 3.0 * inner)


def split_at(value, hi, lo, row, col):
    top = value.astype(BF16)
    rows = slice(row, row + value.shape[0])
    cols = slice(col, col + value.shape[1])
    hi[rows, cols] = top
    lo[rows, cols] = (value - top.astype(F32)).astype(BF16)


def x_rows(ybuf, c, rows, weights, hi, lo, at):
    for start in range(0, 64, 16):
        for h in range(2):
            parts = [ybuf[c, r, h, start : start + 16] for r in rows]
            ones = [p for p, w in zip(parts, weights) if w == 1]
            threes = [p for p, w in zip(parts, weights) if w == 3]
            value = sum(ones[1:], ones[0]) if ones else None
            if threes:
                heavy = 3.0 * sum(threes[1:], threes[0])
                value = heavy if value is None else value + heavy
            split_at(value, hi, lo, at + start, 128 * h)


def linear_kernel(void_hbm, slip_hbm, class_hbm, v_ref, even_ref, odd_ref, fields, class_ref, ybuf, hi, lo, wbuf, pad2, pad3, classes, sems, class_sem):
    parity = lax.axis_index("blk") % 2
    pairs = ROWS // 2

    def copies(k):
        rows = pl.ds(2 * k, 2)
        y = pl.ds(LEAD, NY)
        out = []
        for h in range(2):
            z = pl.ds(128 * h, 128)
            out.append(pltpu.make_async_copy(void_hbm.at[rows, :, z], fields.at[0, rows, h, y], sems.at[k, h]))
            out.append(pltpu.make_async_copy(slip_hbm.at[:, rows, :, z], fields.at[pl.ds(1, 3), rows, h, y], sems.at[k, 2 + h]))
        return out

    class_copy = pltpu.make_async_copy(class_hbm, classes, class_sem)
    class_copy.start()
    for k in range(pairs):
        for copy in copies(k):
            copy.start()
    for c in range(4):
        for row in (0, ROWS + 1):
            for h in range(2):
                ybuf[c, row, h] = jnp.zeros((64, 128), F32)
    table = restrict_z(NZ)
    table_lo = restrict_z(128, 128, 0)
    table_hi = restrict_z(128, 128, 64)
    table3 = [restrict_z(64, 128, 32 * c) for c in range(4)]
    class_copy.wait()
    class_ref[...] = classes[...].astype(F32)

    def along_y(k):
        for copy in copies(k):
            copy.wait()
        for c in range(4):
            for r in range(2):
                row = 2 * k + r
                for h in range(2):
                    wrap_plane(fields, (c, row, h), NY)

                def put(h, start, value):
                    ybuf[c, row + 1, h, start : start + 16] = value

                y_rows(lambda h: fields.at[c, row, h], LEAD, put, 64)

    def along_x(i, at):
        base = 2 * i
        for c in range(4):
            x_rows(ybuf, c, (base, base + 1, base + 2, base + 3), (1, 3, 3, 1), hi, lo, at + 64 * c)
        out = dot2(hi[at : at + 256], lo[at : at + 256], table)
        for c in range(4):
            v_ref[c, i] = out[c * 64 : c * 64 + 64]

    along_y(0)

    def body(i, carry):
        along_y(i + 1)
        along_x(i, 0)
        return carry

    lax.fori_loop(0, pairs - 1, body, 0)
    along_x(pairs - 1, 0)

    def side_rows(ref, last, at):
        r0 = jnp.where(last == 1, ROWS, 1)
        r1 = jnp.where(last == 1, ROWS - 1, 2)
        r2 = jnp.where(last == 1, ROWS - 2, 3)
        for c in range(4):
            x_rows(ybuf, c, (r0,), (1,), hi, lo, at + 64 * c)
            x_rows(ybuf, c, (r0, r1, r2), (3, 3, 1), hi, lo, at + 256 + 64 * c)
        ref[0:512] = dot2(hi[at : at + 512], lo[at : at + 512], table)

    side_rows(even_ref, 1 - parity, 256)
    side_rows(odd_ref, parity, 768)

    table2 = restrict_z(128)
    for m in range(2):
        for c in range(4):
            fill_pad(
                pad2,
                4 * m + c,
                lambda s, t: (v_ref[c, 2 * m + 1, pl.ds(s, t)] + v_ref[c, 2 * m + 4, pl.ds(s, t)])
                + 3.0 * (v_ref[c, 2 * m + 2, pl.ds(s, t)] + v_ref[c, 2 * m + 3, pl.ds(s, t)]),
                64,
                32,
                128,
            )
            restrict_y(pad2, 4 * m + c, 64, hi, lo, 32 * (4 * m + c), 128)
    out = dot2(hi[0:256, 0:128], lo[0:256, 0:128], table2)
    for m in range(2):
        for c in range(4):
            wbuf[c, m] = out[32 * (4 * m + c) : 32 * (4 * m + c) + 32]

    def side_levels(ref, last, slot):
        n1 = jnp.where(last == 1, 6, 1)
        n2 = jnp.where(last == 1, 5, 2)
        at = 256 + 128 * slot
        for c in range(4):
            p = 8 + 4 * slot + c
            fill_pad(pad2, p, lambda s, t: 3.0 * v_ref[c, n1, pl.ds(s, t)] + v_ref[c, n2, pl.ds(s, t)], 64, 32, 128)
            restrict_y(pad2, p, 64, hi, lo, at + 32 * c, 128)
        for half in range(2):
            row = at + 64 * half
            ref[512 + 32 * half : 544 + 32 * half] = dot2(
                hi[row : row + 32, 0:128], lo[row : row + 32, 0:128], table_lo
            ) + dot2(hi[row + 32 : row + 64, 0:128], lo[row + 32 : row + 64, 0:128], table_hi)
        m1 = jnp.where(last == 1, 1, 0)
        m2 = jnp.where(last == 1, 0, 1)
        at = 512 + 64 * slot
        for c in range(4):
            p = 4 * slot + c
            fill_pad(pad3, p, lambda s, t: 3.0 * wbuf[c, m1, pl.ds(s, t)] + wbuf[c, m2, pl.ds(s, t)], 32, 32, 64)
            restrict_y(pad3, p, 32, hi, lo, at + 16 * c, 64)
        total = jnp.zeros((16, 128), F32)
        for c in range(4):
            row = at + 16 * c
            total = total + dot2(hi[row : row + 16, 0:64], lo[row : row + 16, 0:64], table3[c])
        ref[576:592] = total
        outer = jnp.where(last == 1, class_ref[1], class_ref[0])
        ref[592:608] = jnp.concatenate([outer, jnp.zeros((16, 96), F32)], axis=1)

    side_levels(even_ref, 1 - parity, 0)
    side_levels(odd_ref, parity, 1)


def wrap_plane(ref, index, rows):
    plane = ref.at[index]
    plane[LEAD - 1 : LEAD] = plane[LEAD + rows - 1 : LEAD + rows]
    plane[LEAD + rows : LEAD + rows + 1] = plane[LEAD : LEAD + 1]


def linear_call(void, slip, classes):
    hbm = pl.BlockSpec(memory_space=pltpu.HBM)
    vmem = pl.BlockSpec(memory_space=pltpu.VMEM)
    return pl.pallas_call(
        linear_kernel,
        out_shape=(
            jax.ShapeDtypeStruct((4, 8, 64, 128), F32),
            jax.ShapeDtypeStruct((608, 128), F32),
            jax.ShapeDtypeStruct((608, 128), F32),
            jax.ShapeDtypeStruct((4, ROWS, 2, NY + 16, 128), F32),
            jax.ShapeDtypeStruct((2, 16, 32), F32),
        ),
        in_specs=[hbm, hbm, hbm],
        out_specs=(vmem,) * 5,
        scratch_shapes=[
            pltpu.VMEM((4, ROWS + 2, 2, 64, 128), F32),
            pltpu.VMEM((1280, NZ), BF16),
            pltpu.VMEM((1280, NZ), BF16),
            pltpu.VMEM((4, 2, 32, 64), F32),
            pltpu.VMEM((16, 64 + 16, 128), F32),
            pltpu.VMEM((8, 32 + 16, 128), F32),
            pltpu.VMEM((2, 16, 32), jnp.int32),
            pltpu.SemaphoreType.DMA((8, 4)),
            pltpu.SemaphoreType.DMA,
        ],
        compiler_params=pltpu.CompilerParams(vmem_limit_bytes=12 << 20),
        name="linear_part",
    )(void, slip, classes)


def drag_kernel(fields, class_ref, scale_ref, g_ref, filt_ref, edge_ref, kappa, ybuf, hi, lo):
    pairs = ROWS // 2
    for c in range(3):
        for row in (0, ROWS + 1):
            for h in range(2):
                ybuf[c, row, h] = jnp.zeros((64, 128), F32)
    for b in range(2):
        kappa[b] = class_factor(scale_ref, spread(class_ref[b], 16, NZ))
    table = restrict_z(NZ)

    def drag_rows(k):
        block = k // 4
        for r in range(2):
            x = 2 * k + r
            for y in range(16):
                rows = slice(LEAD + 8 * y, LEAD + 8 * y + 8)
                for h in range(2):
                    factor = jnp.broadcast_to(kappa[block, y : y + 1, 128 * h : 128 * h + 128], (8, 128))
                    g = drag(*(fields[c, x, h, rows] for c in range(4)), factor)
                    for c in range(3):
                        g_ref[c, x, h, rows] = g[c]
            for c in range(3):
                for h in range(2):
                    wrap_plane(g_ref, (c, x, h), NY)

    def along_y(k):
        for c in range(3):
            for r in range(2):
                row = 2 * k + r

                def put(h, start, value):
                    ybuf[c, row + 1, h, start : start + 16] = value

                y_rows(lambda h: g_ref.at[c, row, h], LEAD, put, 64)

    def along_x(i, at):
        base = 2 * i
        for c in range(3):
            x_rows(ybuf, c, (base, base + 1, base + 2, base + 3), (1, 3, 3, 1), hi, lo, at + 64 * c)
        out = dot2(hi[at : at + 192], lo[at : at + 192], table)
        for c in range(3):
            filt_ref[c, i] = out[c * 64 : c * 64 + 64]

    drag_rows(0)
    drag_rows(1)
    along_y(0)

    def body(i, carry):
        drag_rows(i + 2)
        along_y(i + 1)
        along_x(i, 0)
        return carry

    lax.fori_loop(0, pairs - 2, body, 0)
    along_y(pairs - 1)
    along_x(pairs - 2, 0)
    along_x(pairs - 1, 192)
    for e, row in enumerate((1, ROWS)):
        at = 384 + 192 * e
        for c in range(3):
            x_rows(ybuf, c, (row,), (1,), hi, lo, at + 64 * c)
        out = dot2(hi[at : at + 192], lo[at : at + 192], table)
        for c in range(3):
            edge_ref[e, c] = out[c * 64 : c * 64 + 64]


def drag_call(fields, classes, scale):
    vmem = pl.BlockSpec(memory_space=pltpu.VMEM)
    return pl.pallas_call(
        drag_kernel,
        out_shape=(
            jax.ShapeDtypeStruct((3, ROWS, 2, NY + 16, 128), F32),
            jax.ShapeDtypeStruct((3, 8, 64, 128), F32),
            jax.ShapeDtypeStruct((2, 3, 64, 128), F32),
        ),
        in_specs=[vmem, vmem, pl.BlockSpec(memory_space=pltpu.SMEM)],
        out_specs=(vmem,) * 3,
        scratch_shapes=[
            pltpu.VMEM((2, 16, NZ), F32),
            pltpu.VMEM((3, ROWS + 2, 2, 64, 128), F32),
            pltpu.VMEM((768, NZ), BF16),
            pltpu.VMEM((768, NZ), BF16),
        ],
        compiler_params=pltpu.CompilerParams(vmem_limit_bytes=10 << 20),
        cost_estimate=pl.CostEstimate(flops=60_000_000, bytes_accessed=16_000_000, transcendentals=1_500_000),
        name="drag_part",
    )(fields, classes, scale)


def x_prolong(planes, count):
    for f in range(-1, 2 * count + 1):
        centre = (f >> 1) + 1
        beside = centre + (1 if f & 1 else -1)
        yield f + 1, 3.0 * planes(centre) + planes(beside)


def plain_prolong_z(length):
    coarse = iota((length, 2 * length), 0)
    fine = iota((length, 2 * length), 1)
    centre = lax.shift_right_logical(fine, 1)
    neighbour = jnp.clip(centre - 1 + 2 * (fine & 1), 0, length - 1)
    return (jnp.where(coarse == centre, 3.0, 0.0) + jnp.where(coarse == neighbour, 1.0, 0.0)).astype(BF16)


def prolong_levels(g1_ref, g2_ref, g3_ref, wide_ref, table_ref, pad3, up3, pad2, up2, pad1):
    first = plain_prolong_z(128)
    second = jnp.dot(plain_prolong_z(64), first, preferred_element_type=F32)
    third = jnp.dot(plain_prolong_z(32), plain_prolong_z(64), preferred_element_type=F32)
    third = jnp.dot(third.astype(BF16), first, preferred_element_type=F32)
    table_ref[0:128] = (first.astype(F32) * (1.0 / 64.0)).astype(BF16)
    table_ref[128:192] = (second * (1.0 / 64.0**2)).astype(BF16)
    table_ref[192:224] = (third * (1.0 / 64.0**3)).astype(BF16)
    table_ref[224:256] = jnp.zeros((32, NZ), BF16)
    for c in range(3):
        for e in range(4):
            p = 4 * c + e
            pad3[p, LEAD : LEAD + 16, 0:32] = g3_ref[c, e]
            wrap_rows(pad3, p, 16)
            prolong_y(pad3, p, 16, up3, p)
        for f, value in x_prolong(lambda e: up3[4 * c + e], 2):
            both = jnp.concatenate([g2_ref[c, f], value[:, 0:32], jnp.zeros((32, 32), F32)], axis=1)
            p = 6 * c + f
            pad2[p, LEAD : LEAD + 32] = both
            wrap_rows(pad2, p, 32)
            prolong_y(pad2, p, 32, up2, p)
        for f, value in x_prolong(lambda e: up2[6 * c + e], 4):
            p = 10 * c + f
            for h, part in enumerate((g1_ref[c, f], value)):
                q = 2 * p + h
                pad1[q, LEAD : LEAD + 64] = part
                wrap_rows(pad1, q, 64)
                prolong_y(pad1, q, 64, wide_ref, q)


def levels_kernel(
    v_in, even_own, odd_own, even_in, odd_in, filt_ref, edge_ref, class_ref, scale_ref,
    wide_ref, table_ref, sums_ref,
    v, w, g1_ref, g2_ref, g3_ref, gpad, pad, hi, lo, kap, pad3, up3, pad2, up2, pad1,
):
    parity = lax.axis_index("blk") % 2
    is_even = parity == 0

    def left(rows):
        return jnp.where(is_even, odd_in[rows], even_in[rows])

    def right(rows):
        return jnp.where(is_even, even_in[rows], odd_in[rows])

    def own_first(rows):
        return jnp.where(is_even, odd_own[rows], even_own[rows])

    def own_last(rows):
        return jnp.where(is_even, even_own[rows], odd_own[rows])

    for c in range(4):
        outer = slice(64 * c, 64 * c + 64)
        combined = slice(256 + 64 * c, 256 + 64 * c + 64)
        v[c, 0] = left(combined) + own_first(outer)
        v[c, 1] = v_in[c, 0] + left(outer)
        for i in range(1, 7):
            v[c, i + 1] = v_in[c, i]
        v[c, 8] = v_in[c, 7] + right(outer)
        v[c, 9] = right(combined) + own_last(outer)
    blocks = [
        left(slice(592, 608))[:, 0:32],
        class_ref[0],
        class_ref[1],
        right(slice(592, 608))[:, 0:32],
    ]
    for b in range(4):
        kap[b] = class_factor(scale_ref, spread(blocks[b], 64, 128))
    numerator = jnp.zeros((64, 128), F32)
    denominator = jnp.zeros((64, 128), F32)
    for i in range(10):
        slips = v[1, i], v[2, i], v[3, i]
        g = drag(v[0, i], *slips, kap[(i + 3) // 4])
        for c in range(3):
            g1_ref[c, i] = g[c]
            if i == 0:
                numerator += edge_ref[0, c] * slips[c]
            elif i == 9:
                numerator += edge_ref[1, c] * slips[c]
            else:
                numerator += filt_ref[c, i - 1] * slips[c]
                denominator += g[c] * slips[c]
    sums = [jnp.sum(numerator, axis=0, keepdims=True), jnp.sum(denominator, axis=0, keepdims=True)]

    table2 = restrict_z(128)

    def x_part(src, c, i, count):
        def part(start, step):
            rows = pl.ds(start, step)
            if i == -1:
                return 3.0 * src[c, 0, rows] + src[c, 1, rows]
            if i == count:
                return src[c, 2 * count, rows] + 3.0 * src[c, 2 * count + 1, rows]
            return (src[c, 2 * i, rows] + src[c, 2 * i + 3, rows]) + 3.0 * (
                src[c, 2 * i + 1, rows] + src[c, 2 * i + 2, rows]
            )

        return part

    n = 0
    for i in range(-1, 5):
        for c in range(4):
            fill_pad(pad, n, x_part(v, c, i, 4), 64, 32, 128)
            restrict_y(pad, n, 64, hi, lo, 32 * n, 128)
            n += 1
    for i in range(4):
        for c in range(3):
            fill_pad(pad, n, x_part(g1_ref, c, i, 4), 64, 32, 128)
            restrict_y(pad, n, 64, hi, lo, 32 * n, 128)
            n += 1
    out = dot2(hi[0 : 32 * n, 0:128], lo[0 : 32 * n, 0:128], table2)
    for i in range(6):
        for c in range(4):
            value = out[32 * (4 * i + c) : 32 * (4 * i + c) + 32]
            if i == 0 or i == 5:
                rows = slice(512 + 32 * (c // 2), 544 + 32 * (c // 2))
                beyond = left(rows) if i == 0 else right(rows)
                if c % 2:
                    beyond = pltpu.roll(beyond, 64, 1)
                value = value + beyond[:, 0:64]
            w[c, i] = value
    numerator = jnp.zeros((32, 64), F32)
    denominator = jnp.zeros((32, 64), F32)
    factors = [class_factor(scale_ref, spread(block, 32, 64)) for block in blocks]
    for i in range(6):
        slips = w[1, i], w[2, i], w[3, i]
        g = drag(w[0, i], *slips, factors[(i + 1) // 2])
        for c in range(3):
            g2_ref[c, i] = g[c]
            if 1 <= i <= 4:
                at = 32 * (24 + 3 * (i - 1) + c)
                numerator += out[at : at + 32] * slips[c]
                denominator += g[c] * slips[c]
    sums += [jnp.sum(numerator, axis=0, keepdims=True), jnp.sum(denominator, axis=0, keepdims=True)]

    table3 = restrict_z(64)
    n = 0
    for i in range(-1, 3):
        for c in range(4):
            fill_pad(gpad, n, x_part(w, c, i, 2), 32, 32, 64)
            restrict_y(gpad, n, 32, hi, lo, 16 * n, 64)
            n += 1
    for i in range(2):
        for c in range(3):
            fill_pad(gpad, n, x_part(g2_ref, c, i, 2), 32, 32, 64)
            restrict_y(gpad, n, 32, hi, lo, 16 * n, 64)
            n += 1
    out = dot2(hi[0 : 16 * n, 0:64], lo[0 : 16 * n, 0:64], table3)
    numerator = jnp.zeros((16, 32), F32)
    denominator = jnp.zeros((16, 32), F32)
    for i in range(4):
        channels = []
        for c in range(4):
            value = out[16 * (4 * i + c) : 16 * (4 * i + c) + 16]
            if i == 0 or i == 3:
                beyond = left(slice(576, 592)) if i == 0 else right(slice(576, 592))
                if c:
                    beyond = pltpu.roll(beyond, 128 - 32 * c, 1)
                value = value + beyond[:, 0:32]
            channels.append(value)
        g = drag(*channels, class_factor(scale_ref, blocks[i]))
        for c in range(3):
            g3_ref[c, i] = g[c]
            if 1 <= i <= 2:
                at = 16 * (16 + 3 * (i - 1) + c)
                numerator += out[at : at + 16] * channels[c + 1]
                denominator += g[c] * channels[c + 1]
    sums += [jnp.sum(numerator, axis=0, keepdims=True), jnp.sum(denominator, axis=0, keepdims=True)]
    ones = jnp.ones((1, 32), F32)
    packed = [sums[0], sums[1]] + [jnp.concatenate([sums[2 + k], sums[4 + k], ones], axis=1) for k in range(2)]
    tile = jnp.concatenate(packed + [jnp.zeros((4, 128), F32)], axis=0)
    for d in range(16):
        sums_ref[d] = tile
    prolong_levels(g1_ref, g2_ref, g3_ref, wide_ref, table_ref, pad3, up3, pad2, up2, pad1)


def levels_call(v_part, even_own, odd_own, even_in, odd_in, filt, edge, classes, scale):
    vmem = pl.BlockSpec(memory_space=pltpu.VMEM)
    return pl.pallas_call(
        levels_kernel,
        out_shape=(
            jax.ShapeDtypeStruct((60, NY, 128), F32),
            jax.ShapeDtypeStruct((256, NZ), BF16),
            jax.ShapeDtypeStruct((16, 8, 128), F32),
        ),
        in_specs=[vmem] * 8 + [pl.BlockSpec(memory_space=pltpu.SMEM)],
        out_specs=(vmem,) * 3,
        scratch_shapes=[
            pltpu.VMEM((4, 10, 64, 128), F32),
            pltpu.VMEM((4, 6, 32, 64), F32),
            pltpu.VMEM((3, 10, 64, 128), F32),
            pltpu.VMEM((3, 6, 32, 64), F32),
            pltpu.VMEM((3, 4, 16, 32), F32),
            pltpu.VMEM((22, 32 + 16, 128), F32),
            pltpu.VMEM((36, 64 + 16, 128), F32),
            pltpu.VMEM((36 * 32, 128), BF16),
            pltpu.VMEM((36 * 32, 128), BF16),
            pltpu.VMEM((4, 64, 128), F32),
            pltpu.VMEM((12, 16 + 16, 128), F32),
            pltpu.VMEM((12, 32, 128), F32),
            pltpu.VMEM((18, 32 + 16, 128), F32),
            pltpu.VMEM((18, 64, 128), F32),
            pltpu.VMEM((60, 64 + 16, 128), F32),
        ],
        compiler_params=pltpu.CompilerParams(vmem_limit_bytes=14 << 20),
        name="small_levels",
    )(v_part, even_own, odd_own, even_in, odd_in, filt, edge, classes, scale)


def final_kernel(sums_ref, wide_ref, table_ref, g0_ref, out_hbm, stage, hi, lo, fine, sems):
    total = jnp.sum(sums_ref[...], axis=0)
    ratios = [total[2 * h : 2 * h + 1] / total[2 * h + 1 : 2 * h + 2] - 1.0 for h in range(2)]

    def make_fine(e):
        slot = e % 2
        for c in range(3):
            for h in range(2):
                for start in range(0, NY, 16):
                    value = wide_ref[20 * c + 2 * e + h, start : start + 16] * ratios[h]
                    split_at(value, hi.at[slot], lo.at[slot], NY * c + start, 128 * h)
        for c in range(3):
            rows = slice(NY * c, NY * c + NY)
            fine[e, c] = dot2(hi[slot, rows], lo[slot, rows], table_ref[...])

    def out_copy(step):
        rows = pl.ds(2 * step, 2)
        return pltpu.make_async_copy(stage.at[:, rows], out_hbm.at[:, rows], sems.at[step])

    for e in range(3):
        make_fine(e)
    for step in range(8):
        if step < 7:
            make_fine(step + 3)
        for c in range(3):
            for h in range(2):
                cols = slice(128 * h, 128 * h + 128)
                for start in range(0, NY, 16):
                    rows = slice(start, start + 16)
                    lead = slice(LEAD + start, LEAD + start + 16)
                    centre = 3.0 * fine[step + 1, c, rows, cols]
                    low = g0_ref[c, 2 * step, h, lead] + (centre + fine[step, c, rows, cols])
                    high = g0_ref[c, 2 * step + 1, h, lead] + (centre + fine[step + 2, c, rows, cols])
                    stage[c, 2 * step, rows, cols] = low
                    stage[c, 2 * step + 1, rows, cols] = high
        out_copy(step).start()
    for step in range(8):
        out_copy(step).wait()


def final_call(sums, wide, table, g0):
    vmem = pl.BlockSpec(memory_space=pltpu.VMEM)
    return pl.pallas_call(
        final_kernel,
        out_shape=jax.ShapeDtypeStruct((3, ROWS, NY, NZ), F32),
        in_specs=[vmem] * 4,
        out_specs=pl.BlockSpec(memory_space=pltpu.HBM),
        scratch_shapes=[
            pltpu.VMEM((3, ROWS, NY, NZ), F32),
            pltpu.VMEM((2, 3 * NY, NZ), BF16),
            pltpu.VMEM((2, 3 * NY, NZ), BF16),
            pltpu.VMEM((10, 3, NY, NZ), F32),
            pltpu.SemaphoreType.DMA((8,)),
        ],
        compiler_params=pltpu.CompilerParams(vmem_limit_bytes=16 << 20),
        name="final_part",
    )(sums, wide, table, g0)


def shards(void_fraction, slip_velocity, size_class, class_scale):
    count = lax.axis_size("blk")
    even_pairs = [(i, i ^ 1) for i in range(count)]
    odd_pairs = [(i, (i + 1) % count if i % 2 else (i - 1) % count) for i in range(count)]
    void_fraction, slip_velocity, size_class = (
        pltpu.with_memory_space_constraint(x, pltpu.HBM) for x in (void_fraction, slip_velocity, size_class)
    )
    v_part, even_own, odd_own, fields, classes = linear_call(void_fraction, slip_velocity, size_class)
    odd_in = lax.ppermute(odd_own, "blk", odd_pairs)
    even_in = lax.ppermute(even_own, "blk", even_pairs)
    g0, filt, edge = drag_call(fields, classes, class_scale)
    wide, table, sums = levels_call(
        v_part, even_own, odd_own, even_in, odd_in, filt, edge, classes, class_scale
    )
    sums = lax.all_to_all(sums, "blk", 0, 0)
    return final_call(sums, wide, table, g0)


def solution(mesh):
    return jax.shard_map(
        shards,
        mesh=mesh,
        in_specs=(P("blk", None, "grp"), P(None, "blk", None, "grp"), P("blk", None, "grp"), P()),
        out_specs=P(None, "blk", None, "grp"),
        check_vma=False,
    )
```

```python
import math

import jax
import jax.numpy as jnp
from jax import lax
from jax.experimental import pallas as pl
from jax.experimental.pallas import tpu as pltpu
from jax.sharding import PartitionSpec as P


F32 = jnp.float32
BF16 = jnp.bfloat16
ROWS = 16
NY = 128
NZ = 256
LEAD = 8
TINY = 1.1754944e-38
POWER = -1.65 * math.log2(math.e)


def iota(shape, axis):
    return lax.broadcasted_iota(jnp.int32, shape, axis)


def restrict_z(length, width=None, shift=0):
    width = width or length // 2
    fine = iota((length, width), 0)
    coarse = iota((length, width), 1) - shift
    offset = fine - 2 * coarse
    weight = jnp.where((offset == 0) | (offset == 1), 3.0, 0.0)
    weight = weight + jnp.where((offset == -1) | (offset == 2), 1.0, 0.0)
    weight = weight + jnp.where((fine == 0) & (coarse == 0), 1.0, 0.0)
    last = length // 2 - 1
    weight = weight + jnp.where((fine == length - 1) & (coarse == last), 1.0, 0.0)
    weight = jnp.where((coarse >= 0) & (coarse <= last), weight, 0.0)
    return (weight * (1.0 / 512.0)).astype(BF16)


def spread(values, rows, lanes):
    a, b = values.shape
    along = (iota((b, lanes), 0) == iota((b, lanes), 1) // (lanes // b)).astype(BF16)
    wide = jnp.dot(values.astype(BF16), along, preferred_element_type=F32)
    if rows == a:
        return wide
    down = (iota((rows, a), 1) == iota((rows, a), 0) // (rows // a)).astype(BF16)
    return jnp.dot(down, wide.astype(BF16), preferred_element_type=F32)


def class_factor(scale_ref, classes):
    chosen = jnp.where(classes < 0.5, scale_ref[0], scale_ref[1])
    chosen = jnp.where(classes < 1.5, chosen, scale_ref[2])
    return jnp.where(classes < 2.5, chosen, scale_ref[3])


def drag(void, s0, s1, s2, kappa):
    square = s0 * s0 + s1 * s1 + s2 * s2
    speed = square * lax.rsqrt(jnp.maximum(square, TINY))
    factor = (kappa * (1.0 - void)) * (jnp.exp2(POWER * jnp.log(void)) * speed)
    return factor * s0, factor * s1, factor * s2


def dot2(hi, lo, table):
    return jnp.dot(hi, table, preferred_element_type=F32) + jnp.dot(
        lo, table, preferred_element_type=F32
    )


def wrap_rows(pad, q, rows):
    pad[q, LEAD - 1 : LEAD] = pad[q, LEAD + rows - 1 : LEAD + rows]
    pad[q, LEAD + rows : LEAD + rows + 1] = pad[q, LEAD : LEAD + 1]


def fill_pad(pad, p, part, rows, step, lanes):
    planes = -(-lanes // 128)
    for start in range(0, rows, step):
        value = part(start, step)
        rng = slice(LEAD + start, LEAD + start + step)
        if lanes < 128:
            pad[p, rng, 0:lanes] = value
        else:
            for h in range(planes):
                pad[planes * p + h, rng] = value[:, 128 * h : 128 * h + 128]
    for h in range(planes):
        wrap_rows(pad, planes * p + h, rows)


def restrict_y(pad, p, rows, hi_ref, lo_ref, out_start, lanes, step=16):
    half = rows // 2
    step = min(step, half)
    planes = -(-lanes // 128)
    width = min(lanes, 128)
    for start in range(0, half, step):
        for h in range(planes):
            at = LEAD + 2 * start
            q = planes * p + h
            outer = pad[q, pl.ds(at - 1, step, stride=2), :] + pad[q, pl.ds(at + 2, step, stride=2), :]
            inner = pad[q, pl.ds(at, step, stride=2), :] + pad[q, pl.ds(at + 1, step, stride=2), :]
            value = (outer + 3.0 * inner)[:, 0:width]
            hi = value.astype(BF16)
            rng = slice(out_start + start, out_start + start + step)
            cols = slice(128 * h, 128 * h + width)
            hi_ref[rng, cols] = hi
            lo_ref[rng, cols] = (value - hi.astype(F32)).astype(BF16)


def prolong_y(pad, p, rows, wide, q):
    step = min(rows, 32)
    for start in range(0, rows, step):
        at = LEAD + start
        centre = 3.0 * pad[p, at : at + step]
        wide[q, pl.ds(2 * start, step, stride=2), :] = centre + pad[p, at - 1 : at - 1 + step]
        wide[q, pl.ds(2 * start + 1, step, stride=2), :] = centre + pad[p, at + 1 : at + 1 + step]


def y_rows(src, lead, dst, half_rows):
    for start in range(0, half_rows, 16):
        for h in range(2):
            at = lead + 2 * start
            plane = src(h)
            outer = plane[pl.ds(at - 1, 16, stride=2), :] + plane[pl.ds(at + 2, 16, stride=2), :]
            inner = plane[pl.ds(at, 16, stride=2), :] + plane[pl.ds(at + 1, 16, stride=2), :]
            dst(h, start, outer + 3.0 * inner)


def split_at(value, hi, lo, row, col):
    top = value.astype(BF16)
    rows = slice(row, row + value.shape[0])
    cols = slice(col, col + value.shape[1])
    hi[rows, cols] = top
    lo[rows, cols] = (value - top.astype(F32)).astype(BF16)


def x_rows(ybuf, c, rows, weights, hi, lo, at):
    for start in range(0, 64, 16):
        for h in range(2):
            parts = [ybuf[c, r, h, start : start + 16] for r in rows]
            ones = [p for p, w in zip(parts, weights) if w == 1]
            threes = [p for p, w in zip(parts, weights) if w == 3]
            value = sum(ones[1:], ones[0]) if ones else None
            if threes:
                heavy = 3.0 * sum(threes[1:], threes[0])
                value = heavy if value is None else value + heavy
            split_at(value, hi, lo, at + start, 128 * h)


def linear_kernel(void_hbm, slip_hbm, class_hbm, v_ref, even_ref, odd_ref, fields, class_ref, ybuf, hi, lo, wbuf, pad2, pad3, classes, sems, class_sem):
    parity = lax.axis_index("blk") % 2

    def copies(k):
        rows = pl.ds(2 * k, 2)
        y = pl.ds(LEAD, NY)
        out = []
        for h in range(2):
            z = pl.ds(128 * h, 128)
            out.append(pltpu.make_async_copy(void_hbm.at[rows, :, z], fields.at[0, rows, h, y], sems.at[k, h]))
            out.append(pltpu.make_async_copy(slip_hbm.at[:, rows, :, z], fields.at[pl.ds(1, 3), rows, h, y], sems.at[k, 2 + h]))
        return out

    class_copy = pltpu.make_async_copy(class_hbm, classes, class_sem)
    class_copy.start()
    order = (0, 7, 1, 6, 2, 5, 3, 4)
    for k in order:
        for copy in copies(k):
            copy.start()
    for c in range(4):
        for row in (0, ROWS + 1):
            for h in range(2):
                ybuf[c, row, h] = jnp.zeros((64, 128), F32)
    table = restrict_z(NZ)
    table_lo = restrict_z(128, 128, 0)
    table_hi = restrict_z(128, 128, 64)
    table3 = [restrict_z(64, 128, 32 * c) for c in range(4)]
    class_copy.wait()
    class_ref[...] = classes[...].astype(F32)

    def along_y(k):
        for copy in copies(k):
            copy.wait()
        for c in range(4):
            for r in range(2):
                row = 2 * k + r
                for h in range(2):
                    wrap_plane(fields, (c, row, h), NY)

                def put(h, start, value):
                    ybuf[c, row + 1, h, start : start + 16] = value

                y_rows(lambda h: fields.at[c, row, h], LEAD, put, 64)

    def along_x(i, at):
        base = 2 * i
        for c in range(4):
            x_rows(ybuf, c, (base, base + 1, base + 2, base + 3), (1, 3, 3, 1), hi, lo, at + 64 * c)
        out = dot2(hi[at : at + 256], lo[at : at + 256], table)
        for c in range(4):
            v_ref[c, i] = out[c * 64 : c * 64 + 64]

    def side_rows(ref, last, at):
        r0 = jnp.where(last == 1, ROWS, 1)
        r1 = jnp.where(last == 1, ROWS - 1, 2)
        r2 = jnp.where(last == 1, ROWS - 2, 3)
        for c in range(4):
            x_rows(ybuf, c, (r0,), (1,), hi, lo, at + 64 * c)
            x_rows(ybuf, c, (r0, r1, r2), (3, 3, 1), hi, lo, at + 256 + 64 * c)
        ref[0:512] = dot2(hi[at : at + 512], lo[at : at + 512], table)

    for k in order[:4]:
        along_y(k)
    along_x(0, 0)
    along_x(7, 256 * 7)
    side_rows(even_ref, 1 - parity, 2048)
    side_rows(odd_ref, parity, 2560)
    for k, ready in zip(order[4:], ((1,), (6,), (2,), (3, 4, 5))):
        along_y(k)
        for i in ready:
            along_x(i, 256 * i)

    table2 = restrict_z(128)
    for m in range(2):
        for c in range(4):
            fill_pad(
                pad2,
                4 * m + c,
                lambda s, t: (v_ref[c, 2 * m + 1, pl.ds(s, t)] + v_ref[c, 2 * m + 4, pl.ds(s, t)])
                + 3.0 * (v_ref[c, 2 * m + 2, pl.ds(s, t)] + v_ref[c, 2 * m + 3, pl.ds(s, t)]),
                64,
                32,
                128,
            )
            restrict_y(pad2, 4 * m + c, 64, hi, lo, 32 * (4 * m + c), 128)
    out = dot2(hi[0:256, 0:128], lo[0:256, 0:128], table2)
    for m in range(2):
        for c in range(4):
            wbuf[c, m] = out[32 * (4 * m + c) : 32 * (4 * m + c) + 32]

    def side_levels(ref, last, slot):
        n1 = jnp.where(last == 1, 6, 1)
        n2 = jnp.where(last == 1, 5, 2)
        at = 256 + 128 * slot
        for c in range(4):
            p = 8 + 4 * slot + c
            fill_pad(pad2, p, lambda s, t: 3.0 * v_ref[c, n1, pl.ds(s, t)] + v_ref[c, n2, pl.ds(s, t)], 64, 32, 128)
            restrict_y(pad2, p, 64, hi, lo, at + 32 * c, 128)
        for half in range(2):
            row = at + 64 * half
            ref[512 + 32 * half : 544 + 32 * half] = dot2(
                hi[row : row + 32, 0:128], lo[row : row + 32, 0:128], table_lo
            ) + dot2(hi[row + 32 : row + 64, 0:128], lo[row + 32 : row + 64, 0:128], table_hi)
        m1 = jnp.where(last == 1, 1, 0)
        m2 = jnp.where(last == 1, 0, 1)
        at = 512 + 64 * slot
        for c in range(4):
            p = 4 * slot + c
            fill_pad(pad3, p, lambda s, t: 3.0 * wbuf[c, m1, pl.ds(s, t)] + wbuf[c, m2, pl.ds(s, t)], 32, 32, 64)
            restrict_y(pad3, p, 32, hi, lo, at + 16 * c, 64)
        total = jnp.zeros((16, 128), F32)
        for c in range(4):
            row = at + 16 * c
            total = total + dot2(hi[row : row + 16, 0:64], lo[row : row + 16, 0:64], table3[c])
        ref[576:592] = total
        outer = jnp.where(last == 1, class_ref[1], class_ref[0])
        ref[592:608] = jnp.concatenate([outer, jnp.zeros((16, 96), F32)], axis=1)

    side_levels(even_ref, 1 - parity, 0)
    side_levels(odd_ref, parity, 1)


def wrap_plane(ref, index, rows):
    plane = ref.at[index]
    plane[LEAD - 1 : LEAD] = plane[LEAD + rows - 1 : LEAD + rows]
    plane[LEAD + rows : LEAD + rows + 1] = plane[LEAD : LEAD + 1]


def linear_call(void, slip, classes):
    hbm = pl.BlockSpec(memory_space=pltpu.HBM)
    vmem = pl.BlockSpec(memory_space=pltpu.VMEM)
    return pl.pallas_call(
        linear_kernel,
        out_shape=(
            jax.ShapeDtypeStruct((4, 8, 64, 128), F32),
            jax.ShapeDtypeStruct((608, 128), F32),
            jax.ShapeDtypeStruct((608, 128), F32),
            jax.ShapeDtypeStruct((4, ROWS, 2, NY + 16, 128), F32),
            jax.ShapeDtypeStruct((2, 16, 32), F32),
        ),
        in_specs=[hbm, hbm, hbm],
        out_specs=(vmem,) * 5,
        scratch_shapes=[
            pltpu.VMEM((4, ROWS + 2, 2, 64, 128), F32),
            pltpu.VMEM((3072, NZ), BF16),
            pltpu.VMEM((3072, NZ), BF16),
            pltpu.VMEM((4, 2, 32, 64), F32),
            pltpu.VMEM((16, 64 + 16, 128), F32),
            pltpu.VMEM((8, 32 + 16, 128), F32),
            pltpu.VMEM((2, 16, 32), jnp.int32),
            pltpu.SemaphoreType.DMA((8, 4)),
            pltpu.SemaphoreType.DMA,
        ],
        compiler_params=pltpu.CompilerParams(vmem_limit_bytes=14 << 20),
        name="linear_part",
    )(void, slip, classes)


def drag_kernel(fields, class_ref, scale_ref, g_ref, filt_ref, edge_ref, kappa, ybuf, hi, lo):
    pairs = ROWS // 2
    for c in range(3):
        for row in (0, ROWS + 1):
            for h in range(2):
                ybuf[c, row, h] = jnp.zeros((64, 128), F32)
    for b in range(2):
        kappa[b] = class_factor(scale_ref, spread(class_ref[b], 16, NZ))
    table = restrict_z(NZ)

    def drag_rows(k):
        block = k // 4
        for r in range(2):
            x = 2 * k + r
            for y in range(16):
                rows = slice(LEAD + 8 * y, LEAD + 8 * y + 8)
                for h in range(2):
                    factor = jnp.broadcast_to(kappa[block, y : y + 1, 128 * h : 128 * h + 128], (8, 128))
                    g = drag(*(fields[c, x, h, rows] for c in range(4)), factor)
                    for c in range(3):
                        g_ref[c, x, h, rows] = g[c]
            for c in range(3):
                for h in range(2):
                    wrap_plane(g_ref, (c, x, h), NY)

    def along_y(k):
        for c in range(3):
            for r in range(2):
                row = 2 * k + r

                def put(h, start, value):
                    ybuf[c, row + 1, h, start : start + 16] = value

                y_rows(lambda h: g_ref.at[c, row, h], LEAD, put, 64)

    def along_x(i, at):
        base = 2 * i
        for c in range(3):
            x_rows(ybuf, c, (base, base + 1, base + 2, base + 3), (1, 3, 3, 1), hi, lo, at + 64 * c)
        out = dot2(hi[at : at + 192], lo[at : at + 192], table)
        for c in range(3):
            filt_ref[c, i] = out[c * 64 : c * 64 + 64]

    drag_rows(0)
    drag_rows(1)
    along_y(0)

    def body(i, carry):
        drag_rows(i + 2)
        along_y(i + 1)
        along_x(i, 0)
        return carry

    lax.fori_loop(0, pairs - 2, body, 0)
    along_y(pairs - 1)
    along_x(pairs - 2, 0)
    along_x(pairs - 1, 192)
    for e, row in enumerate((1, ROWS)):
        at = 384 + 192 * e
        for c in range(3):
            x_rows(ybuf, c, (row,), (1,), hi, lo, at + 64 * c)
        out = dot2(hi[at : at + 192], lo[at : at + 192], table)
        for c in range(3):
            edge_ref[e, c] = out[c * 64 : c * 64 + 64]


def drag_call(fields, classes, scale):
    vmem = pl.BlockSpec(memory_space=pltpu.VMEM)
    return pl.pallas_call(
        drag_kernel,
        out_shape=(
            jax.ShapeDtypeStruct((3, ROWS, 2, NY + 16, 128), F32),
            jax.ShapeDtypeStruct((3, 8, 64, 128), F32),
            jax.ShapeDtypeStruct((2, 3, 64, 128), F32),
        ),
        in_specs=[vmem, vmem, pl.BlockSpec(memory_space=pltpu.SMEM)],
        out_specs=(vmem,) * 3,
        scratch_shapes=[
            pltpu.VMEM((2, 16, NZ), F32),
            pltpu.VMEM((3, ROWS + 2, 2, 64, 128), F32),
            pltpu.VMEM((768, NZ), BF16),
            pltpu.VMEM((768, NZ), BF16),
        ],
        compiler_params=pltpu.CompilerParams(vmem_limit_bytes=10 << 20),
        cost_estimate=pl.CostEstimate(flops=60_000_000, bytes_accessed=16_000_000, transcendentals=1_500_000),
        name="drag_part",
    )(fields, classes, scale)


def x_prolong(planes, count):
    for f in range(-1, 2 * count + 1):
        centre = (f >> 1) + 1
        beside = centre + (1 if f & 1 else -1)
        yield f + 1, 3.0 * planes(centre) + planes(beside)


def plain_prolong_z(length):
    coarse = iota((length, 2 * length), 0)
    fine = iota((length, 2 * length), 1)
    centre = lax.shift_right_logical(fine, 1)
    neighbour = jnp.clip(centre - 1 + 2 * (fine & 1), 0, length - 1)
    return (jnp.where(coarse == centre, 3.0, 0.0) + jnp.where(coarse == neighbour, 1.0, 0.0)).astype(BF16)


def make_table(table_ref):
    first = plain_prolong_z(128)
    second = jnp.dot(plain_prolong_z(64), first, preferred_element_type=F32)
    third = jnp.dot(plain_prolong_z(32), plain_prolong_z(64), preferred_element_type=F32)
    third = jnp.dot(third.astype(BF16), first, preferred_element_type=F32)
    table_ref[0:128] = (first.astype(F32) * (1.0 / 64.0)).astype(BF16)
    table_ref[128:192] = (second * (1.0 / 64.0**2)).astype(BF16)
    table_ref[192:224] = (third * (1.0 / 64.0**3)).astype(BF16)
    table_ref[224:256] = jnp.zeros((32, NZ), BF16)


def put_wide(pad, q, part, wide, to):
    pad[q, LEAD : LEAD + 64] = part
    wrap_rows(pad, q, 64)
    prolong_y(pad, q, 64, wide, to)


def x_part(plane, c, i, count):
    def part(start, step):
        rows = pl.ds(start, step)
        if i == -1:
            return 3.0 * plane(c, -1)[rows] + plane(c, 0)[rows]
        if i == count:
            return plane(c, 2 * count - 1)[rows] + 3.0 * plane(c, 2 * count)[rows]
        return (plane(c, 2 * i - 1)[rows] + plane(c, 2 * i + 2)[rows]) + 3.0 * (
            plane(c, 2 * i)[rows] + plane(c, 2 * i + 1)[rows]
        )

    return part


def total(values):
    return jnp.sum(values, axis=0, keepdims=True)


def inner_kernel(v_in, filt_ref, class_ref, scale_ref, g1_ref, w_ref, g2_ref, wide_ref, table_ref, kap1_ref, kap2_ref, sums_ref, pad, pad1, hi, lo):
    make_table(table_ref)
    for b in range(2):
        kap1_ref[b] = class_factor(scale_ref, spread(class_ref[b], 64, 128))
        kap2_ref[b] = class_factor(scale_ref, spread(class_ref[b], 32, 64))
    numerator = jnp.zeros((64, 128), F32)
    denominator = jnp.zeros((64, 128), F32)
    for i in range(1, 7):
        slips = v_in[1, i], v_in[2, i], v_in[3, i]
        g = drag(v_in[0, i], *slips, kap1_ref[i // 4])
        for c in range(3):
            g1_ref[c, i - 1] = g[c]
            numerator += filt_ref[c, i] * slips[c]
            denominator += g[c] * slips[c]
            put_wide(pad1, 6 * c + i - 1, g[c], wide_ref, 6 * c + i - 1)
    sums_ref[0:1] = total(numerator)
    sums_ref[1:2] = total(denominator)
    n = 0
    for count, plane in ((4, lambda c, i: v_in.at[c, i]), (3, lambda c, i: g1_ref.at[c, i - 1])):
        for i in (1, 2):
            for c in range(count):
                fill_pad(pad, n, x_part(plane, c, i, 4), 64, 32, 128)
                restrict_y(pad, n, 64, hi, lo, 32 * n, 128)
                n += 1
    out = dot2(hi[...], lo[...], restrict_z(128))
    numerator = jnp.zeros((32, 64), F32)
    denominator = jnp.zeros((32, 64), F32)
    for i in (1, 2):
        channels = [out[32 * (4 * (i - 1) + c) : 32 * (4 * (i - 1) + c) + 32] for c in range(4)]
        g = drag(*channels, kap2_ref[i // 2])
        for c in range(4):
            w_ref[c, i - 1] = channels[c]
        for c in range(3):
            g2_ref[c, i - 1] = g[c]
            at = 32 * (8 + 3 * (i - 1) + c)
            numerator += out[at : at + 32] * channels[c + 1]
            denominator += g[c] * channels[c + 1]
    blank = jnp.zeros((1, 64), F32)
    sums_ref[2:3] = jnp.concatenate([total(numerator), blank], axis=1)
    sums_ref[3:4] = jnp.concatenate([total(denominator), blank], axis=1)
    sums_ref[4:8] = jnp.zeros((4, 128), F32)


def inner_call(v_part, filt, classes, scale):
    vmem = pl.BlockSpec(memory_space=pltpu.VMEM)
    return pl.pallas_call(
        inner_kernel,
        out_shape=(
            jax.ShapeDtypeStruct((3, 6, 64, 128), F32),
            jax.ShapeDtypeStruct((4, 2, 32, 64), F32),
            jax.ShapeDtypeStruct((3, 2, 32, 64), F32),
            jax.ShapeDtypeStruct((18, NY, 128), F32),
            jax.ShapeDtypeStruct((256, NZ), BF16),
            jax.ShapeDtypeStruct((2, 64, 128), F32),
            jax.ShapeDtypeStruct((2, 32, 64), F32),
            jax.ShapeDtypeStruct((8, 128), F32),
        ),
        in_specs=[vmem] * 3 + [pl.BlockSpec(memory_space=pltpu.SMEM)],
        out_specs=(vmem,) * 8,
        scratch_shapes=[
            pltpu.VMEM((14, 64 + 16, 128), F32),
            pltpu.VMEM((18, 64 + 16, 128), F32),
            pltpu.VMEM((14 * 32, 128), BF16),
            pltpu.VMEM((14 * 32, 128), BF16),
        ],
        compiler_params=pltpu.CompilerParams(vmem_limit_bytes=8 << 20),
        cost_estimate=pl.CostEstimate(flops=20_000_000, bytes_accessed=4_000_000, transcendentals=300_000),
        name="inner_levels",
    )(v_part, filt, classes, scale)


def levels_kernel(
    v_in, even_own, odd_own, even_in, odd_in, filt_ref, edge_ref, class_ref, scale_ref,
    g1_in, w_in, g2_in, kap1_ref, kap2_ref, part_ref,
    wide_ref, sums_ref,
    v, g1, w, g2, g3, pad, padw, hi, lo, pad3, up3, pad2, up2, pad1,
):
    is_even = lax.axis_index("blk") % 2 == 0

    def left(rows):
        return jnp.where(is_even, odd_in[rows], even_in[rows])

    def right(rows):
        return jnp.where(is_even, even_in[rows], odd_in[rows])

    def own_first(rows):
        return jnp.where(is_even, odd_own[rows], even_own[rows])

    def own_last(rows):
        return jnp.where(is_even, even_own[rows], odd_own[rows])

    slot1 = {-1: 0, 0: 1, 7: 2, 8: 3}
    slot2 = {-1: 0, 0: 1, 3: 2, 4: 3}

    def plane_v(c, i):
        return v.at[c, slot1[i]] if i in slot1 else v_in.at[c, i]

    def plane_g1(c, i):
        return g1.at[c, slot1[i]] if i in slot1 else g1_in.at[c, i - 1]

    def plane_w(c, i):
        return w.at[c, slot2[i]] if i in slot2 else w_in.at[c, i - 1]

    def plane_g2(c, i):
        return g2.at[c, slot2[i]] if i in slot2 else g2_in.at[c, i - 1]

    for c in range(4):
        outer = slice(64 * c, 64 * c + 64)
        combined = slice(256 + 64 * c, 256 + 64 * c + 64)
        v[c, 0] = left(combined) + own_first(outer)
        v[c, 1] = v_in[c, 0] + left(outer)
        v[c, 2] = v_in[c, 7] + right(outer)
        v[c, 3] = right(combined) + own_last(outer)
    beyond = left(slice(592, 608))[:, 0:32], right(slice(592, 608))[:, 0:32]
    factors = {
        -1: class_factor(scale_ref, spread(beyond[0], 64, 128)),
        0: kap1_ref[0],
        7: kap1_ref[1],
        8: class_factor(scale_ref, spread(beyond[1], 64, 128)),
    }
    numerator = jnp.zeros((64, 128), F32)
    denominator = jnp.zeros((64, 128), F32)
    for i, n in slot1.items():
        slips = v[1, n], v[2, n], v[3, n]
        g = drag(v[0, n], *slips, factors[i])
        for c in range(3):
            g1[c, n] = g[c]
            if i == -1:
                numerator += edge_ref[0, c] * slips[c]
            elif i == 8:
                numerator += edge_ref[1, c] * slips[c]
            else:
                numerator += filt_ref[c, i] * slips[c]
                denominator += g[c] * slips[c]
    sums = [total(numerator) + part_ref[0:1], total(denominator) + part_ref[1:2]]

    n = 0
    for count, plane, rows in ((4, plane_v, (-1, 0, 3, 4)), (3, plane_g1, (0, 3))):
        for i in rows:
            for c in range(count):
                fill_pad(pad, n, x_part(plane, c, i, 4), 64, 32, 128)
                restrict_y(pad, n, 64, hi, lo, 32 * n, 128)
                n += 1
    out = dot2(hi[0 : 32 * n, 0:128], lo[0 : 32 * n, 0:128], restrict_z(128))
    factors = {
        -1: class_factor(scale_ref, spread(beyond[0], 32, 64)),
        0: kap2_ref[0],
        3: kap2_ref[1],
        4: class_factor(scale_ref, spread(beyond[1], 32, 64)),
    }
    numerator = jnp.zeros((32, 64), F32)
    denominator = jnp.zeros((32, 64), F32)
    for i, n in slot2.items():
        channels = []
        for c in range(4):
            value = out[32 * (4 * n + c) : 32 * (4 * n + c) + 32]
            if i in (-1, 4):
                rows = slice(512 + 32 * (c // 2), 544 + 32 * (c // 2))
                more = left(rows) if i == -1 else right(rows)
                if c % 2:
                    more = pltpu.roll(more, 64, 1)
                value = value + more[:, 0:64]
            w[c, n] = value
            channels.append(value)
        g = drag(*channels, factors[i])
        for c in range(3):
            g2[c, n] = g[c]
            if i in (0, 3):
                at = 32 * (16 + 3 * (n - 1) + c)
                numerator += out[at : at + 32] * channels[c + 1]
                denominator += g[c] * channels[c + 1]
    sums += [total(numerator) + part_ref[2:3, 0:64], total(denominator) + part_ref[3:4, 0:64]]

    n = 0
    for count, plane, rows in ((4, plane_w, (-1, 0, 1, 2)), (3, plane_g2, (0, 1))):
        for i in rows:
            for c in range(count):
                fill_pad(padw, n, x_part(plane, c, i, 2), 32, 32, 64)
                restrict_y(padw, n, 32, hi, lo, 16 * n, 64)
                n += 1
    out = dot2(hi[0 : 16 * n, 0:64], lo[0 : 16 * n, 0:64], restrict_z(64))
    numerator = jnp.zeros((16, 32), F32)
    denominator = jnp.zeros((16, 32), F32)
    blocks = [beyond[0], class_ref[0], class_ref[1], beyond[1]]
    for i in range(4):
        channels = []
        for c in range(4):
            value = out[16 * (4 * i + c) : 16 * (4 * i + c) + 16]
            if i == 0 or i == 3:
                more = left(slice(576, 592)) if i == 0 else right(slice(576, 592))
                if c:
                    more = pltpu.roll(more, 128 - 32 * c, 1)
                value = value + more[:, 0:32]
            channels.append(value)
        g = drag(*channels, class_factor(scale_ref, blocks[i]))
        for c in range(3):
            g3[c, i] = g[c]
            if 1 <= i <= 2:
                at = 16 * (16 + 3 * (i - 1) + c)
                numerator += out[at : at + 16] * channels[c + 1]
                denominator += g[c] * channels[c + 1]
    sums += [total(numerator), total(denominator)]
    ones = jnp.ones((1, 32), F32)
    packed = [sums[0], sums[1]] + [jnp.concatenate([sums[2 + k], sums[4 + k], ones], axis=1) for k in range(2)]
    tile = jnp.concatenate(packed + [jnp.zeros((4, 128), F32)], axis=0)
    for d in range(16):
        sums_ref[d] = tile

    for c in range(3):
        for e in range(4):
            p = 4 * c + e
            pad3[p, LEAD : LEAD + 16, 0:32] = g3[c, e]
            wrap_rows(pad3, p, 16)
            prolong_y(pad3, p, 16, up3, p)
        for f, value in x_prolong(lambda e: up3[4 * c + e], 2):
            p = 6 * c + f
            pad2[p, LEAD : LEAD + 32] = jnp.concatenate(
                [plane_g2(c, f - 1)[...], value[:, 0:32], jnp.zeros((32, 32), F32)], axis=1
            )
            wrap_rows(pad2, p, 32)
            prolong_y(pad2, p, 32, up2, p)
        for f, value in x_prolong(lambda e: up2[6 * c + e], 4):
            put_wide(pad1, 10 * c + f, value, wide_ref, 10 * c + f)
        for n in slot1.values():
            put_wide(pad1, 30 + 4 * c + n, g1[c, n], wide_ref, 30 + 4 * c + n)


def levels_call(v_part, even_own, odd_own, even_in, odd_in, filt, edge, classes, scale, g1, w, g2, kap1, kap2, part):
    vmem = pl.BlockSpec(memory_space=pltpu.VMEM)
    return pl.pallas_call(
        levels_kernel,
        out_shape=(
            jax.ShapeDtypeStruct((42, NY, 128), F32),
            jax.ShapeDtypeStruct((16, 8, 128), F32),
        ),
        in_specs=[vmem] * 8 + [pl.BlockSpec(memory_space=pltpu.SMEM)] + [vmem] * 6,
        out_specs=(vmem,) * 2,
        scratch_shapes=[
            pltpu.VMEM((4, 4, 64, 128), F32),
            pltpu.VMEM((3, 4, 64, 128), F32),
            pltpu.VMEM((4, 4, 32, 64), F32),
            pltpu.VMEM((3, 4, 32, 64), F32),
            pltpu.VMEM((3, 4, 16, 32), F32),
            pltpu.VMEM((22, 64 + 16, 128), F32),
            pltpu.VMEM((22, 32 + 16, 128), F32),
            pltpu.VMEM((22 * 32, 128), BF16),
            pltpu.VMEM((22 * 32, 128), BF16),
            pltpu.VMEM((12, 16 + 16, 128), F32),
            pltpu.VMEM((12, 32, 128), F32),
            pltpu.VMEM((18, 32 + 16, 128), F32),
            pltpu.VMEM((18, 64, 128), F32),
            pltpu.VMEM((42, 64 + 16, 128), F32),
        ],
        compiler_params=pltpu.CompilerParams(vmem_limit_bytes=12 << 20),
        name="small_levels",
    )(v_part, even_own, odd_own, even_in, odd_in, filt, edge, classes, scale, g1, w, g2, kap1, kap2, part)


def final_kernel(sums_ref, inner_ref, wide_ref, table_ref, g0_ref, out_hbm, stage, hi, lo, fine, sems):
    added = jnp.sum(sums_ref[...], axis=0)
    ratios = [added[2 * h : 2 * h + 1] / added[2 * h + 1 : 2 * h + 2] - 1.0 for h in range(2)]

    def wide(c, e, h):
        if h:
            return wide_ref.at[10 * c + e]
        if 2 <= e <= 7:
            return inner_ref.at[6 * c + e - 2]
        return wide_ref.at[30 + 4 * c + {0: 0, 1: 1, 8: 2, 9: 3}[e]]

    def make_fine(e):
        slot = e % 2
        for c in range(3):
            for h in range(2):
                for start in range(0, NY, 16):
                    value = wide(c, e, h)[start : start + 16] * ratios[h]
                    split_at(value, hi.at[slot], lo.at[slot], NY * c + start, 128 * h)
        for c in range(3):
            rows = slice(NY * c, NY * c + NY)
            fine[e, c] = dot2(hi[slot, rows], lo[slot, rows], table_ref[...])

    def out_copy(step):
        rows = pl.ds(2 * step, 2)
        return pltpu.make_async_copy(stage.at[:, rows], out_hbm.at[:, rows], sems.at[step])

    for e in range(3):
        make_fine(e)
    for step in range(8):
        if step < 7:
            make_fine(step + 3)
        for c in range(3):
            for h in range(2):
                cols = slice(128 * h, 128 * h + 128)
                for start in range(0, NY, 16):
                    rows = slice(start, start + 16)
                    lead = slice(LEAD + start, LEAD + start + 16)
                    centre = 3.0 * fine[step + 1, c, rows, cols]
                    low = g0_ref[c, 2 * step, h, lead] + (centre + fine[step, c, rows, cols])
                    high = g0_ref[c, 2 * step + 1, h, lead] + (centre + fine[step + 2, c, rows, cols])
                    stage[c, 2 * step, rows, cols] = low
                    stage[c, 2 * step + 1, rows, cols] = high
        out_copy(step).start()
    for step in range(8):
        out_copy(step).wait()


def final_call(sums, inner, wide, table, g0):
    vmem = pl.BlockSpec(memory_space=pltpu.VMEM)
    return pl.pallas_call(
        final_kernel,
        out_shape=jax.ShapeDtypeStruct((3, ROWS, NY, NZ), F32),
        in_specs=[vmem] * 5,
        out_specs=pl.BlockSpec(memory_space=pltpu.HBM),
        scratch_shapes=[
            pltpu.VMEM((3, ROWS, NY, NZ), F32),
            pltpu.VMEM((2, 3 * NY, NZ), BF16),
            pltpu.VMEM((2, 3 * NY, NZ), BF16),
            pltpu.VMEM((10, 3, NY, NZ), F32),
            pltpu.SemaphoreType.DMA((8,)),
        ],
        compiler_params=pltpu.CompilerParams(vmem_limit_bytes=16 << 20),
        name="final_part",
    )(sums, inner, wide, table, g0)


def shards(void_fraction, slip_velocity, size_class, class_scale):
    count = lax.axis_size("blk")
    even_pairs = [(i, i ^ 1) for i in range(count)]
    odd_pairs = [(i, (i + 1) % count if i % 2 else (i - 1) % count) for i in range(count)]
    void_fraction, slip_velocity, size_class = (
        pltpu.with_memory_space_constraint(x, pltpu.HBM) for x in (void_fraction, slip_velocity, size_class)
    )
    v_part, even_own, odd_own, fields, classes = linear_call(void_fraction, slip_velocity, size_class)
    odd_in = lax.ppermute(odd_own, "blk", odd_pairs)
    even_in = lax.ppermute(even_own, "blk", even_pairs)
    g0, filt, edge = drag_call(fields, classes, class_scale)
    g1, w, g2, inner, table, kap1, kap2, part = inner_call(v_part, filt, classes, class_scale)
    wide, sums = levels_call(
        v_part, even_own, odd_own, even_in, odd_in, filt, edge, classes, class_scale, g1, w, g2, kap1, kap2, part
    )
    sums = lax.all_to_all(sums, "blk", 0, 0)
    return final_call(sums, inner, wide, table, g0)


def solution(mesh):
    return jax.shard_map(
        shards,
        mesh=mesh,
        in_specs=(P("blk", None, "grp"), P(None, "blk", None, "grp"), P("blk", None, "grp"), P()),
        out_specs=P(None, "blk", None, "grp"),
        check_vma=False,
    )
```

```python
import math

import jax
import jax.numpy as jnp
from jax import lax
from jax.experimental import pallas as pl
from jax.experimental.pallas import tpu as pltpu
from jax.sharding import PartitionSpec as P


F32 = jnp.float32
BF16 = jnp.bfloat16
ROWS = 16
NY = 128
NZ = 256
LEAD = 8
TINY = 1.1754944e-38
POWER = -1.65 * math.log2(math.e)


def iota(shape, axis):
    return lax.broadcasted_iota(jnp.int32, shape, axis)


def restrict_z(length, width=None, shift=0):
    width = width or length // 2
    fine = iota((length, width), 0)
    coarse = iota((length, width), 1) - shift
    offset = fine - 2 * coarse
    weight = jnp.where((offset == 0) | (offset == 1), 3.0, 0.0)
    weight = weight + jnp.where((offset == -1) | (offset == 2), 1.0, 0.0)
    weight = weight + jnp.where((fine == 0) & (coarse == 0), 1.0, 0.0)
    last = length // 2 - 1
    weight = weight + jnp.where((fine == length - 1) & (coarse == last), 1.0, 0.0)
    weight = jnp.where((coarse >= 0) & (coarse <= last), weight, 0.0)
    return (weight * (1.0 / 512.0)).astype(BF16)


def spread(values, rows, lanes):
    a, b = values.shape
    along = (iota((b, lanes), 0) == iota((b, lanes), 1) // (lanes // b)).astype(BF16)
    wide = jnp.dot(values.astype(BF16), along, preferred_element_type=F32)
    if rows == a:
        return wide
    down = (iota((rows, a), 1) == iota((rows, a), 0) // (rows // a)).astype(BF16)
    return jnp.dot(down, wide.astype(BF16), preferred_element_type=F32)


def class_factor(scale_ref, classes):
    chosen = jnp.where(classes < 0.5, scale_ref[0], scale_ref[1])
    chosen = jnp.where(classes < 1.5, chosen, scale_ref[2])
    return jnp.where(classes < 2.5, chosen, scale_ref[3])


def drag(void, s0, s1, s2, kappa):
    square = s0 * s0 + s1 * s1 + s2 * s2
    speed = square * lax.rsqrt(jnp.maximum(square, TINY))
    factor = (kappa * (1.0 - void)) * (jnp.exp2(POWER * jnp.log(void)) * speed)
    return factor * s0, factor * s1, factor * s2


def dot2(hi, lo, table):
    if hi.shape[1] % 128 == 0:
        both = jnp.concatenate([hi, lo], axis=1)
        return jnp.dot(both, jnp.concatenate([table, table], axis=0), preferred_element_type=F32)
    return jnp.dot(hi, table, preferred_element_type=F32) + jnp.dot(
        lo, table, preferred_element_type=F32
    )


def wrap_rows(pad, q, rows):
    pad[q, LEAD - 1 : LEAD] = pad[q, LEAD + rows - 1 : LEAD + rows]
    pad[q, LEAD + rows : LEAD + rows + 1] = pad[q, LEAD : LEAD + 1]


def fill_pad(pad, p, part, rows, step, lanes):
    planes = -(-lanes // 128)
    for start in range(0, rows, step):
        value = part(start, step)
        rng = slice(LEAD + start, LEAD + start + step)
        if lanes < 128:
            pad[p, rng, 0:lanes] = value
        else:
            for h in range(planes):
                pad[planes * p + h, rng] = value[:, 128 * h : 128 * h + 128]
    for h in range(planes):
        wrap_rows(pad, planes * p + h, rows)


def restrict_y(pad, p, rows, hi_ref, lo_ref, out_start, lanes, step=16):
    half = rows // 2
    step = min(step, half)
    planes = -(-lanes // 128)
    width = min(lanes, 128)
    for start in range(0, half, step):
        for h in range(planes):
            at = LEAD + 2 * start
            q = planes * p + h
            outer = pad[q, pl.ds(at - 1, step, stride=2), :] + pad[q, pl.ds(at + 2, step, stride=2), :]
            inner = pad[q, pl.ds(at, step, stride=2), :] + pad[q, pl.ds(at + 1, step, stride=2), :]
            value = (outer + 3.0 * inner)[:, 0:width]
            hi = value.astype(BF16)
            rng = slice(out_start + start, out_start + start + step)
            cols = slice(128 * h, 128 * h + width)
            hi_ref[rng, cols] = hi
            lo_ref[rng, cols] = (value - hi.astype(F32)).astype(BF16)


def prolong_y(pad, p, rows, wide, q):
    step = min(rows, 32)
    for start in range(0, rows, step):
        at = LEAD + start
        centre = 3.0 * pad[p, at : at + step]
        wide[q, pl.ds(2 * start, step, stride=2), :] = centre + pad[p, at - 1 : at - 1 + step]
        wide[q, pl.ds(2 * start + 1, step, stride=2), :] = centre + pad[p, at + 1 : at + 1 + step]


def y_rows(src, lead, dst, half_rows):
    for start in range(0, half_rows, 16):
        for h in range(2):
            at = lead + 2 * start
            plane = src(h)
            outer = plane[pl.ds(at - 1, 16, stride=2), :] + plane[pl.ds(at + 2, 16, stride=2), :]
            inner = plane[pl.ds(at, 16, stride=2), :] + plane[pl.ds(at + 1, 16, stride=2), :]
            dst(h, start, outer + 3.0 * inner)


def split_at(value, hi, lo, row, col):
    top = value.astype(BF16)
    rows = slice(row, row + value.shape[0])
    cols = slice(col, col + value.shape[1])
    hi[rows, cols] = top
    lo[rows, cols] = (value - top.astype(F32)).astype(BF16)


def x_rows(ybuf, c, rows, weights, hi, lo, at):
    for start in range(0, 64, 16):
        for h in range(2):
            parts = [ybuf[c, r, h, start : start + 16] for r in rows]
            ones = [p for p, w in zip(parts, weights) if w == 1]
            threes = [p for p, w in zip(parts, weights) if w == 3]
            value = sum(ones[1:], ones[0]) if ones else None
            if threes:
                heavy = 3.0 * sum(threes[1:], threes[0])
                value = heavy if value is None else value + heavy
            split_at(value, hi, lo, at + start, 128 * h)


def linear_kernel(void_hbm, slip_hbm, class_hbm, v_ref, even_ref, odd_ref, fields, class_ref, ybuf, hi, lo, wbuf, pad2, pad3, classes, sems, class_sem):
    parity = lax.axis_index("blk") % 2

    def copies(k):
        rows = pl.ds(2 * k, 2)
        y = pl.ds(LEAD, NY)
        out = []
        for h in range(2):
            z = pl.ds(128 * h, 128)
            out.append(pltpu.make_async_copy(void_hbm.at[rows, :, z], fields.at[0, rows, h, y], sems.at[k, h]))
            out.append(pltpu.make_async_copy(slip_hbm.at[:, rows, :, z], fields.at[pl.ds(1, 3), rows, h, y], sems.at[k, 2 + h]))
        return out

    class_copy = pltpu.make_async_copy(class_hbm, classes, class_sem)
    class_copy.start()
    order = (0, 7, 1, 6, 2, 5, 3, 4)
    for k in order:
        for copy in copies(k):
            copy.start()
    for c in range(4):
        for row in (0, ROWS + 1):
            for h in range(2):
                ybuf[c, row, h] = jnp.zeros((64, 128), F32)
    table = restrict_z(NZ)
    table_lo = restrict_z(128, 128, 0)
    table_hi = restrict_z(128, 128, 64)
    table3 = [restrict_z(64, 128, 32 * c) for c in range(4)]
    class_copy.wait()
    class_ref[...] = classes[...].astype(F32)

    def along_y(k):
        for copy in copies(k):
            copy.wait()
        for c in range(4):
            for r in range(2):
                row = 2 * k + r
                for h in range(2):
                    wrap_plane(fields, (c, row, h), NY)

                def put(h, start, value):
                    ybuf[c, row + 1, h, start : start + 16] = value

                y_rows(lambda h: fields.at[c, row, h], LEAD, put, 64)

    def along_x(i, at):
        base = 2 * i
        for c in range(4):
            x_rows(ybuf, c, (base, base + 1, base + 2, base + 3), (1, 3, 3, 1), hi, lo, at + 64 * c)
        out = dot2(hi[at : at + 256], lo[at : at + 256], table)
        for c in range(4):
            v_ref[c, i] = out[c * 64 : c * 64 + 64]

    def side_rows(ref, last, at):
        r0 = jnp.where(last == 1, ROWS, 1)
        r1 = jnp.where(last == 1, ROWS - 1, 2)
        r2 = jnp.where(last == 1, ROWS - 2, 3)
        for c in range(4):
            x_rows(ybuf, c, (r0,), (1,), hi, lo, at + 64 * c)
            x_rows(ybuf, c, (r0, r1, r2), (3, 3, 1), hi, lo, at + 256 + 64 * c)
        ref[0:512] = dot2(hi[at : at + 512], lo[at : at + 512], table)

    for k in order[:4]:
        along_y(k)
    for k, ready in zip(order[4:], ((0, 7), (1,), (6,), (2, 3, 4, 5))):
        along_y(k)
        if k == 5:
            side_rows(odd_ref, parity, 2560)
        if k == 3:
            side_rows(even_ref, 1 - parity, 2048)
        for i in ready:
            along_x(i, 256 * i)

    table2 = restrict_z(128)
    for m in range(2):
        for c in range(4):
            fill_pad(
                pad2,
                4 * m + c,
                lambda s, t: (v_ref[c, 2 * m + 1, pl.ds(s, t)] + v_ref[c, 2 * m + 4, pl.ds(s, t)])
                + 3.0 * (v_ref[c, 2 * m + 2, pl.ds(s, t)] + v_ref[c, 2 * m + 3, pl.ds(s, t)]),
                64,
                32,
                128,
            )
            restrict_y(pad2, 4 * m + c, 64, hi, lo, 32 * (4 * m + c), 128)
    out = dot2(hi[0:256, 0:128], lo[0:256, 0:128], table2)
    for m in range(2):
        for c in range(4):
            wbuf[c, m] = out[32 * (4 * m + c) : 32 * (4 * m + c) + 32]

    def side_levels(ref, last, slot):
        n1 = jnp.where(last == 1, 6, 1)
        n2 = jnp.where(last == 1, 5, 2)
        at = 256 + 128 * slot
        for c in range(4):
            p = 8 + 4 * slot + c
            fill_pad(pad2, p, lambda s, t: 3.0 * v_ref[c, n1, pl.ds(s, t)] + v_ref[c, n2, pl.ds(s, t)], 64, 32, 128)
            restrict_y(pad2, p, 64, hi, lo, at + 32 * c, 128)
        for half in range(2):
            row = at + 64 * half
            ref[512 + 32 * half : 544 + 32 * half] = dot2(
                hi[row : row + 32, 0:128], lo[row : row + 32, 0:128], table_lo
            ) + dot2(hi[row + 32 : row + 64, 0:128], lo[row + 32 : row + 64, 0:128], table_hi)
        m1 = jnp.where(last == 1, 1, 0)
        m2 = jnp.where(last == 1, 0, 1)
        at = 512 + 64 * slot
        for c in range(4):
            p = 4 * slot + c
            fill_pad(pad3, p, lambda s, t: 3.0 * wbuf[c, m1, pl.ds(s, t)] + wbuf[c, m2, pl.ds(s, t)], 32, 32, 64)
            restrict_y(pad3, p, 32, hi, lo, at + 16 * c, 64)
        total = jnp.zeros((16, 128), F32)
        for c in range(4):
            row = at + 16 * c
            total = total + dot2(hi[row : row + 16, 0:64], lo[row : row + 16, 0:64], table3[c])
        ref[576:592] = total
        outer = jnp.where(last == 1, class_ref[1], class_ref[0])
        ref[592:608] = jnp.concatenate([outer, jnp.zeros((16, 96), F32)], axis=1)

    side_levels(even_ref, 1 - parity, 0)
    side_levels(odd_ref, parity, 1)


def wrap_plane(ref, index, rows):
    plane = ref.at[index]
    plane[LEAD - 1 : LEAD] = plane[LEAD + rows - 1 : LEAD + rows]
    plane[LEAD + rows : LEAD + rows + 1] = plane[LEAD : LEAD + 1]


def linear_call(void, slip, classes):
    hbm = pl.BlockSpec(memory_space=pltpu.HBM)
    vmem = pl.BlockSpec(memory_space=pltpu.VMEM)
    return pl.pallas_call(
        linear_kernel,
        out_shape=(
            jax.ShapeDtypeStruct((4, 8, 64, 128), F32),
            jax.ShapeDtypeStruct((608, 128), F32),
            jax.ShapeDtypeStruct((608, 128), F32),
            jax.ShapeDtypeStruct((4, ROWS, 2, NY + 16, 128), F32),
            jax.ShapeDtypeStruct((2, 16, 32), F32),
        ),
        in_specs=[hbm, hbm, hbm],
        out_specs=(vmem,) * 5,
        scratch_shapes=[
            pltpu.VMEM((4, ROWS + 2, 2, 64, 128), F32),
            pltpu.VMEM((3072, NZ), BF16),
            pltpu.VMEM((3072, NZ), BF16),
            pltpu.VMEM((4, 2, 32, 64), F32),
            pltpu.VMEM((16, 64 + 16, 128), F32),
            pltpu.VMEM((8, 32 + 16, 128), F32),
            pltpu.VMEM((2, 16, 32), jnp.int32),
            pltpu.SemaphoreType.DMA((8, 4)),
            pltpu.SemaphoreType.DMA,
        ],
        compiler_params=pltpu.CompilerParams(vmem_limit_bytes=14 << 20),
        name="linear_part",
    )(void, slip, classes)


def drag_kernel(fields, class_ref, scale_ref, g_ref, filt_ref, edge_ref, kappa, ybuf, hi, lo):
    pairs = ROWS // 2
    for c in range(3):
        for row in (0, ROWS + 1):
            for h in range(2):
                ybuf[c, row, h] = jnp.zeros((64, 128), F32)
    for b in range(2):
        kappa[b] = class_factor(scale_ref, spread(class_ref[b], 16, NZ))
    table = restrict_z(NZ)

    def drag_rows(k):
        block = k // 4
        for r in range(2):
            x = 2 * k + r
            for y in range(16):
                rows = slice(LEAD + 8 * y, LEAD + 8 * y + 8)
                for h in range(2):
                    factor = jnp.broadcast_to(kappa[block, y : y + 1, 128 * h : 128 * h + 128], (8, 128))
                    g = drag(*(fields[c, x, h, rows] for c in range(4)), factor)
                    for c in range(3):
                        g_ref[c, x, h, rows] = g[c]
            for c in range(3):
                for h in range(2):
                    wrap_plane(g_ref, (c, x, h), NY)

    def along_y(k):
        for c in range(3):
            for r in range(2):
                row = 2 * k + r

                def put(h, start, value):
                    ybuf[c, row + 1, h, start : start + 16] = value

                y_rows(lambda h: g_ref.at[c, row, h], LEAD, put, 64)

    def along_x(i, at):
        base = 2 * i
        for c in range(3):
            x_rows(ybuf, c, (base, base + 1, base + 2, base + 3), (1, 3, 3, 1), hi, lo, at + 64 * c)
        out = dot2(hi[at : at + 192], lo[at : at + 192], table)
        for c in range(3):
            filt_ref[c, i] = out[c * 64 : c * 64 + 64]

    drag_rows(0)
    drag_rows(1)
    along_y(0)

    def body(i, carry):
        drag_rows(i + 2)
        along_y(i + 1)
        along_x(i, 0)
        return carry

    lax.fori_loop(0, pairs - 2, body, 0)
    along_y(pairs - 1)
    along_x(pairs - 2, 0)
    along_x(pairs - 1, 192)
    for e, row in enumerate((1, ROWS)):
        at = 384 + 192 * e
        for c in range(3):
            x_rows(ybuf, c, (row,), (1,), hi, lo, at + 64 * c)
        out = dot2(hi[at : at + 192], lo[at : at + 192], table)
        for c in range(3):
            edge_ref[e, c] = out[c * 64 : c * 64 + 64]


def drag_call(fields, classes, scale):
    vmem = pl.BlockSpec(memory_space=pltpu.VMEM)
    return pl.pallas_call(
        drag_kernel,
        out_shape=(
            jax.ShapeDtypeStruct((3, ROWS, 2, NY + 16, 128), F32),
            jax.ShapeDtypeStruct((3, 8, 64, 128), F32),
            jax.ShapeDtypeStruct((2, 3, 64, 128), F32),
        ),
        in_specs=[vmem, vmem, pl.BlockSpec(memory_space=pltpu.SMEM)],
        out_specs=(vmem,) * 3,
        scratch_shapes=[
            pltpu.VMEM((2, 16, NZ), F32),
            pltpu.VMEM((3, ROWS + 2, 2, 64, 128), F32),
            pltpu.VMEM((768, NZ), BF16),
            pltpu.VMEM((768, NZ), BF16),
        ],
        compiler_params=pltpu.CompilerParams(vmem_limit_bytes=10 << 20),
        cost_estimate=pl.CostEstimate(flops=60_000_000, bytes_accessed=16_000_000, transcendentals=1_500_000),
        name="drag_part",
    )(fields, classes, scale)


def x_prolong(planes, count):
    for f in range(-1, 2 * count + 1):
        centre = (f >> 1) + 1
        beside = centre + (1 if f & 1 else -1)
        yield f + 1, 3.0 * planes(centre) + planes(beside)


def plain_prolong_z(length):
    coarse = iota((length, 2 * length), 0)
    fine = iota((length, 2 * length), 1)
    centre = lax.shift_right_logical(fine, 1)
    neighbour = jnp.clip(centre - 1 + 2 * (fine & 1), 0, length - 1)
    return (jnp.where(coarse == centre, 3.0, 0.0) + jnp.where(coarse == neighbour, 1.0, 0.0)).astype(BF16)


def make_table(table_ref):
    first = plain_prolong_z(128)
    second = jnp.dot(plain_prolong_z(64), first, preferred_element_type=F32)
    third = jnp.dot(plain_prolong_z(32), plain_prolong_z(64), preferred_element_type=F32)
    third = jnp.dot(third.astype(BF16), first, preferred_element_type=F32)
    table_ref[0:128] = (first.astype(F32) * (1.0 / 64.0)).astype(BF16)
    table_ref[128:192] = (second * (1.0 / 64.0**2)).astype(BF16)
    table_ref[192:224] = (third * (1.0 / 64.0**3)).astype(BF16)
    table_ref[224:256] = jnp.zeros((32, NZ), BF16)


def put_wide(pad, q, part, wide, to):
    pad[q, LEAD : LEAD + 64] = part
    wrap_rows(pad, q, 64)
    prolong_y(pad, q, 64, wide, to)


def x_part(plane, c, i, count):
    def part(start, step):
        rows = pl.ds(start, step)
        if i == -1:
            return 3.0 * plane(c, -1)[rows] + plane(c, 0)[rows]
        if i == count:
            return plane(c, 2 * count - 1)[rows] + 3.0 * plane(c, 2 * count)[rows]
        return (plane(c, 2 * i - 1)[rows] + plane(c, 2 * i + 2)[rows]) + 3.0 * (
            plane(c, 2 * i)[rows] + plane(c, 2 * i + 1)[rows]
        )

    return part


def total(values):
    return jnp.sum(values, axis=0, keepdims=True)


def inner_kernel(v_in, filt_ref, class_ref, scale_ref, g1_ref, w_ref, g2_ref, wide_ref, table_ref, kap1_ref, kap2_ref, sums_ref, pad, pad1, hi, lo):
    make_table(table_ref)
    for b in range(2):
        kap1_ref[b] = class_factor(scale_ref, spread(class_ref[b], 64, 128))
        kap2_ref[b] = class_factor(scale_ref, spread(class_ref[b], 32, 64))
    numerator = jnp.zeros((64, 128), F32)
    denominator = jnp.zeros((64, 128), F32)
    for i in range(1, 7):
        slips = v_in[1, i], v_in[2, i], v_in[3, i]
        g = drag(v_in[0, i], *slips, kap1_ref[i // 4])
        for c in range(3):
            g1_ref[c, i - 1] = g[c]
            numerator += filt_ref[c, i] * slips[c]
            denominator += g[c] * slips[c]
            put_wide(pad1, 6 * c + i - 1, g[c], wide_ref, 6 * c + i - 1)
    sums_ref[0:1] = total(numerator)
    sums_ref[1:2] = total(denominator)
    n = 0
    for count, plane in ((4, lambda c, i: v_in.at[c, i]), (3, lambda c, i: g1_ref.at[c, i - 1])):
        for i in (1, 2):
            for c in range(count):
                fill_pad(pad, n, x_part(plane, c, i, 4), 64, 32, 128)
                restrict_y(pad, n, 64, hi, lo, 32 * n, 128)
                n += 1
    out = dot2(hi[...], lo[...], restrict_z(128))
    numerator = jnp.zeros((32, 64), F32)
    denominator = jnp.zeros((32, 64), F32)
    for i in (1, 2):
        channels = [out[32 * (4 * (i - 1) + c) : 32 * (4 * (i - 1) + c) + 32] for c in range(4)]
        g = drag(*channels, kap2_ref[i // 2])
        for c in range(4):
            w_ref[c, i - 1] = channels[c]
        for c in range(3):
            g2_ref[c, i - 1] = g[c]
            at = 32 * (8 + 3 * (i - 1) + c)
            numerator += out[at : at + 32] * channels[c + 1]
            denominator += g[c] * channels[c + 1]
    blank = jnp.zeros((1, 64), F32)
    sums_ref[2:3] = jnp.concatenate([total(numerator), blank], axis=1)
    sums_ref[3:4] = jnp.concatenate([total(denominator), blank], axis=1)
    sums_ref[4:8] = jnp.zeros((4, 128), F32)


def inner_call(v_part, filt, classes, scale):
    vmem = pl.BlockSpec(memory_space=pltpu.VMEM)
    return pl.pallas_call(
        inner_kernel,
        out_shape=(
            jax.ShapeDtypeStruct((3, 6, 64, 128), F32),
            jax.ShapeDtypeStruct((4, 2, 32, 64), F32),
            jax.ShapeDtypeStruct((3, 2, 32, 64), F32),
            jax.ShapeDtypeStruct((18, NY, 128), F32),
            jax.ShapeDtypeStruct((256, NZ), BF16),
            jax.ShapeDtypeStruct((2, 64, 128), F32),
            jax.ShapeDtypeStruct((2, 32, 64), F32),
            jax.ShapeDtypeStruct((8, 128), F32),
        ),
        in_specs=[vmem] * 3 + [pl.BlockSpec(memory_space=pltpu.SMEM)],
        out_specs=(vmem,) * 8,
        scratch_shapes=[
            pltpu.VMEM((14, 64 + 16, 128), F32),
            pltpu.VMEM((18, 64 + 16, 128), F32),
            pltpu.VMEM((14 * 32, 128), BF16),
            pltpu.VMEM((14 * 32, 128), BF16),
        ],
        compiler_params=pltpu.CompilerParams(vmem_limit_bytes=8 << 20),
        cost_estimate=pl.CostEstimate(flops=20_000_000, bytes_accessed=4_000_000, transcendentals=300_000),
        name="inner_levels",
    )(v_part, filt, classes, scale)


def levels_kernel(
    v_in, even_own, odd_own, even_in, odd_in, filt_ref, edge_ref, class_ref, scale_ref,
    g1_in, w_in, g2_in, kap1_ref, kap2_ref, part_ref,
    wide_ref, sums_ref,
    v, g1, w, g2, g3, pad, padw, hi, lo, pad3, up3, pad2, up2, pad1,
):
    is_even = lax.axis_index("blk") % 2 == 0

    def left(rows):
        return jnp.where(is_even, odd_in[rows], even_in[rows])

    def right(rows):
        return jnp.where(is_even, even_in[rows], odd_in[rows])

    def own_first(rows):
        return jnp.where(is_even, odd_own[rows], even_own[rows])

    def own_last(rows):
        return jnp.where(is_even, even_own[rows], odd_own[rows])

    slot1 = {-1: 0, 0: 1, 7: 2, 8: 3}
    slot2 = {-1: 0, 0: 1, 3: 2, 4: 3}

    def plane_v(c, i):
        return v.at[c, slot1[i]] if i in slot1 else v_in.at[c, i]

    def plane_g1(c, i):
        return g1.at[c, slot1[i]] if i in slot1 else g1_in.at[c, i - 1]

    def plane_w(c, i):
        return w.at[c, slot2[i]] if i in slot2 else w_in.at[c, i - 1]

    def plane_g2(c, i):
        return g2.at[c, slot2[i]] if i in slot2 else g2_in.at[c, i - 1]

    for c in range(4):
        outer = slice(64 * c, 64 * c + 64)
        combined = slice(256 + 64 * c, 256 + 64 * c + 64)
        v[c, 0] = left(combined) + own_first(outer)
        v[c, 1] = v_in[c, 0] + left(outer)
        v[c, 2] = v_in[c, 7] + right(outer)
        v[c, 3] = right(combined) + own_last(outer)
    beyond = left(slice(592, 608))[:, 0:32], right(slice(592, 608))[:, 0:32]
    factors = {
        -1: class_factor(scale_ref, spread(beyond[0], 64, 128)),
        0: kap1_ref[0],
        7: kap1_ref[1],
        8: class_factor(scale_ref, spread(beyond[1], 64, 128)),
    }
    numerator = jnp.zeros((64, 128), F32)
    denominator = jnp.zeros((64, 128), F32)
    for i, n in slot1.items():
        slips = v[1, n], v[2, n], v[3, n]
        g = drag(v[0, n], *slips, factors[i])
        for c in range(3):
            g1[c, n] = g[c]
            if i == -1:
                numerator += edge_ref[0, c] * slips[c]
            elif i == 8:
                numerator += edge_ref[1, c] * slips[c]
            else:
                numerator += filt_ref[c, i] * slips[c]
                denominator += g[c] * slips[c]
    sums = [total(numerator) + part_ref[0:1], total(denominator) + part_ref[1:2]]

    n = 0
    for count, plane, rows in ((4, plane_v, (-1, 0, 3, 4)), (3, plane_g1, (0, 3))):
        for i in rows:
            for c in range(count):
                fill_pad(pad, n, x_part(plane, c, i, 4), 64, 32, 128)
                restrict_y(pad, n, 64, hi, lo, 32 * n, 128)
                n += 1
    out = dot2(hi[0 : 32 * n, 0:128], lo[0 : 32 * n, 0:128], restrict_z(128))
    factors = {
        -1: class_factor(scale_ref, spread(beyond[0], 32, 64)),
        0: kap2_ref[0],
        3: kap2_ref[1],
        4: class_factor(scale_ref, spread(beyond[1], 32, 64)),
    }
    numerator = jnp.zeros((32, 64), F32)
    denominator = jnp.zeros((32, 64), F32)
    for i, n in slot2.items():
        channels = []
        for c in range(4):
            value = out[32 * (4 * n + c) : 32 * (4 * n + c) + 32]
            if i in (-1, 4):
                rows = slice(512 + 32 * (c // 2), 544 + 32 * (c // 2))
                more = left(rows) if i == -1 else right(rows)
                if c % 2:
                    more = pltpu.roll(more, 64, 1)
                value = value + more[:, 0:64]
            w[c, n] = value
            channels.append(value)
        g = drag(*channels, factors[i])
        for c in range(3):
            g2[c, n] = g[c]
            if i in (0, 3):
                at = 32 * (16 + 3 * (n - 1) + c)
                numerator += out[at : at + 32] * channels[c + 1]
                denominator += g[c] * channels[c + 1]
    sums += [total(numerator) + part_ref[2:3, 0:64], total(denominator) + part_ref[3:4, 0:64]]

    n = 0
    for count, plane, rows in ((4, plane_w, (-1, 0, 1, 2)), (3, plane_g2, (0, 1))):
        for i in rows:
            for c in range(count):
                fill_pad(padw, n, x_part(plane, c, i, 2), 32, 32, 64)
                restrict_y(padw, n, 32, hi, lo, 16 * n, 64)
                n += 1
    out = dot2(hi[0 : 16 * n, 0:64], lo[0 : 16 * n, 0:64], restrict_z(64))
    numerator = jnp.zeros((16, 32), F32)
    denominator = jnp.zeros((16, 32), F32)
    blocks = [beyond[0], class_ref[0], class_ref[1], beyond[1]]
    for i in range(4):
        channels = []
        for c in range(4):
            value = out[16 * (4 * i + c) : 16 * (4 * i + c) + 16]
            if i == 0 or i == 3:
                more = left(slice(576, 592)) if i == 0 else right(slice(576, 592))
                if c:
                    more = pltpu.roll(more, 128 - 32 * c, 1)
                value = value + more[:, 0:32]
            channels.append(value)
        g = drag(*channels, class_factor(scale_ref, blocks[i]))
        for c in range(3):
            g3[c, i] = g[c]
            if 1 <= i <= 2:
                at = 16 * (16 + 3 * (i - 1) + c)
                numerator += out[at : at + 16] * channels[c + 1]
                denominator += g[c] * channels[c + 1]
    sums += [total(numerator), total(denominator)]
    ones = jnp.ones((1, 32), F32)
    packed = [sums[0], sums[1]] + [jnp.concatenate([sums[2 + k], sums[4 + k], ones], axis=1) for k in range(2)]
    tile = jnp.concatenate(packed + [jnp.zeros((4, 128), F32)], axis=0)
    for d in range(16):
        sums_ref[d] = tile

    for c in range(3):
        for e in range(4):
            p = 4 * c + e
            pad3[p, LEAD : LEAD + 16, 0:32] = g3[c, e]
            wrap_rows(pad3, p, 16)
            prolong_y(pad3, p, 16, up3, p)
        for f, value in x_prolong(lambda e: up3[4 * c + e], 2):
            p = 6 * c + f
            pad2[p, LEAD : LEAD + 32] = jnp.concatenate(
                [plane_g2(c, f - 1)[...], value[:, 0:32], jnp.zeros((32, 32), F32)], axis=1
            )
            wrap_rows(pad2, p, 32)
            prolong_y(pad2, p, 32, up2, p)
        for f, value in x_prolong(lambda e: up2[6 * c + e], 4):
            put_wide(pad1, 10 * c + f, value, wide_ref, 10 * c + f)
        for n in slot1.values():
            put_wide(pad1, 30 + 4 * c + n, g1[c, n], wide_ref, 30 + 4 * c + n)


def levels_call(v_part, even_own, odd_own, even_in, odd_in, filt, edge, classes, scale, g1, w, g2, kap1, kap2, part):
    vmem = pl.BlockSpec(memory_space=pltpu.VMEM)
    return pl.pallas_call(
        levels_kernel,
        out_shape=(
            jax.ShapeDtypeStruct((42, NY, 128), F32),
            jax.ShapeDtypeStruct((16, 8, 128), F32),
        ),
        in_specs=[vmem] * 8 + [pl.BlockSpec(memory_space=pltpu.SMEM)] + [vmem] * 6,
        out_specs=(vmem,) * 2,
        scratch_shapes=[
            pltpu.VMEM((4, 4, 64, 128), F32),
            pltpu.VMEM((3, 4, 64, 128), F32),
            pltpu.VMEM((4, 4, 32, 64), F32),
            pltpu.VMEM((3, 4, 32, 64), F32),
            pltpu.VMEM((3, 4, 16, 32), F32),
            pltpu.VMEM((22, 64 + 16, 128), F32),
            pltpu.VMEM((22, 32 + 16, 128), F32),
            pltpu.VMEM((22 * 32, 128), BF16),
            pltpu.VMEM((22 * 32, 128), BF16),
            pltpu.VMEM((12, 16 + 16, 128), F32),
            pltpu.VMEM((12, 32, 128), F32),
            pltpu.VMEM((18, 32 + 16, 128), F32),
            pltpu.VMEM((18, 64, 128), F32),
            pltpu.VMEM((42, 64 + 16, 128), F32),
        ],
        compiler_params=pltpu.CompilerParams(vmem_limit_bytes=12 << 20),
        name="small_levels",
    )(v_part, even_own, odd_own, even_in, odd_in, filt, edge, classes, scale, g1, w, g2, kap1, kap2, part)


def final_kernel(sums_ref, inner_ref, wide_ref, table_ref, g0_ref, out_hbm, stage, hi, lo, fine, sems):
    added = jnp.sum(sums_ref[...], axis=0)
    ratios = [added[2 * h : 2 * h + 1] / added[2 * h + 1 : 2 * h + 2] - 1.0 for h in range(2)]

    def wide(c, e, h):
        if h:
            return wide_ref.at[10 * c + e]
        if 2 <= e <= 7:
            return inner_ref.at[6 * c + e - 2]
        return wide_ref.at[30 + 4 * c + {0: 0, 1: 1, 8: 2, 9: 3}[e]]

    def make_fine(e):
        slot = e % 2
        for c in range(3):
            for h in range(2):
                for start in range(0, NY, 16):
                    value = wide(c, e, h)[start : start + 16] * ratios[h]
                    split_at(value, hi.at[slot], lo.at[slot], NY * c + start, 128 * h)
        values = dot2(hi[slot], lo[slot], table_ref[...])
        for c in range(3):
            fine[e, c] = values[NY * c : NY * c + NY]

    def out_copy(row):
        return pltpu.make_async_copy(stage.at[:, row], out_hbm.at[:, row], sems.at[row])

    def make_rows(step, both):
        for c in range(3):
            for h in range(2):
                cols = slice(128 * h, 128 * h + 128)
                for start in range(0, NY, 16):
                    rows = slice(start, start + 16)
                    lead = slice(LEAD + start, LEAD + start + 16)
                    centre = 3.0 * fine[step + 1, c, rows, cols]
                    for half in both:
                        beside = fine[step + 2 * half, c, rows, cols]
                        stage[c, 2 * step + half, rows, cols] = g0_ref[c, 2 * step + half, h, lead] + (centre + beside)
        for half in both:
            out_copy(2 * step + half).start()

    make_fine(0)
    make_fine(1)
    make_fine(2)
    make_rows(0, (0,))
    make_fine(3)
    make_rows(0, (1,))
    for step in range(1, 8):
        if step < 7:
            make_fine(step + 3)
        make_rows(step, (0, 1))
    for row in range(ROWS):
        out_copy(row).wait()


def final_call(sums, inner, wide, table, g0):
    vmem = pl.BlockSpec(memory_space=pltpu.VMEM)
    return pl.pallas_call(
        final_kernel,
        out_shape=jax.ShapeDtypeStruct((3, ROWS, NY, NZ), F32),
        in_specs=[vmem] * 5,
        out_specs=pl.BlockSpec(memory_space=pltpu.HBM),
        scratch_shapes=[
            pltpu.VMEM((3, ROWS, NY, NZ), F32),
            pltpu.VMEM((2, 3 * NY, NZ), BF16),
            pltpu.VMEM((2, 3 * NY, NZ), BF16),
            pltpu.VMEM((10, 3, NY, NZ), F32),
            pltpu.SemaphoreType.DMA((ROWS,)),
        ],
        compiler_params=pltpu.CompilerParams(vmem_limit_bytes=16 << 20),
        name="final_part",
    )(sums, inner, wide, table, g0)


def shards(void_fraction, slip_velocity, size_class, class_scale):
    count = lax.axis_size("blk")
    even_pairs = [(i, i ^ 1) for i in range(count)]
    odd_pairs = [(i, (i + 1) % count if i % 2 else (i - 1) % count) for i in range(count)]
    void_fraction, slip_velocity, size_class = (
        pltpu.with_memory_space_constraint(x, pltpu.HBM) for x in (void_fraction, slip_velocity, size_class)
    )
    v_part, even_own, odd_own, fields, classes = linear_call(void_fraction, slip_velocity, size_class)
    odd_in = lax.ppermute(odd_own, "blk", odd_pairs)
    even_in = lax.ppermute(even_own, "blk", even_pairs)
    g0, filt, edge = drag_call(fields, classes, class_scale)
    g1, w, g2, inner, table, kap1, kap2, part = inner_call(v_part, filt, classes, class_scale)
    wide, sums = levels_call(
        v_part, even_own, odd_own, even_in, odd_in, filt, edge, classes, class_scale, g1, w, g2, kap1, kap2, part
    )
    sums = lax.all_to_all(sums, "blk", 0, 0)
    return final_call(sums, inner, wide, table, g0)


def solution(mesh):
    return jax.shard_map(
        shards,
        mesh=mesh,
        in_specs=(P("blk", None, "grp"), P(None, "blk", None, "grp"), P("blk", None, "grp"), P()),
        out_specs=P(None, "blk", None, "grp"),
        check_vma=False,
    )
```

```python
import math

import jax
import jax.numpy as jnp
from jax import lax
from jax.experimental import pallas as pl
from jax.experimental.pallas import tpu as pltpu
from jax.sharding import PartitionSpec as P


F32 = jnp.float32
BF16 = jnp.bfloat16
ROWS = 16
NY = 128
NZ = 256
LEAD = 8
TINY = 1.1754944e-38
POWER = -1.65 * math.log2(math.e)


def iota(shape, axis):
    return lax.broadcasted_iota(jnp.int32, shape, axis)


def restrict_z(length, width=None, shift=0):
    width = width or length // 2
    fine = iota((length, width), 0)
    coarse = iota((length, width), 1) - shift
    offset = fine - 2 * coarse
    weight = jnp.where((offset == 0) | (offset == 1), 3.0, 0.0)
    weight = weight + jnp.where((offset == -1) | (offset == 2), 1.0, 0.0)
    weight = weight + jnp.where((fine == 0) & (coarse == 0), 1.0, 0.0)
    last = length // 2 - 1
    weight = weight + jnp.where((fine == length - 1) & (coarse == last), 1.0, 0.0)
    weight = jnp.where((coarse >= 0) & (coarse <= last), weight, 0.0)
    return (weight * (1.0 / 512.0)).astype(BF16)


def spread(values, rows, lanes):
    a, b = values.shape
    along = (iota((b, lanes), 0) == iota((b, lanes), 1) // (lanes // b)).astype(BF16)
    wide = jnp.dot(values.astype(BF16), along, preferred_element_type=F32)
    if rows == a:
        return wide
    down = (iota((rows, a), 1) == iota((rows, a), 0) // (rows // a)).astype(BF16)
    return jnp.dot(down, wide.astype(BF16), preferred_element_type=F32)


def class_factor(scale_ref, classes):
    chosen = jnp.where(classes < 0.5, scale_ref[0], scale_ref[1])
    chosen = jnp.where(classes < 1.5, chosen, scale_ref[2])
    return jnp.where(classes < 2.5, chosen, scale_ref[3])


def drag(void, s0, s1, s2, kappa):
    square = s0 * s0 + s1 * s1 + s2 * s2
    speed = square * lax.rsqrt(jnp.maximum(square, TINY))
    factor = (kappa * (1.0 - void)) * (jnp.exp2(POWER * jnp.log(void)) * speed)
    return factor * s0, factor * s1, factor * s2


def dot2(hi, lo, table):
    if hi.shape[1] % 128 == 0:
        both = jnp.concatenate([hi, lo], axis=1)
        return jnp.dot(both, jnp.concatenate([table, table], axis=0), preferred_element_type=F32)
    return jnp.dot(hi, table, preferred_element_type=F32) + jnp.dot(
        lo, table, preferred_element_type=F32
    )


def wrap_rows(pad, q, rows):
    pad[q, LEAD - 1 : LEAD] = pad[q, LEAD + rows - 1 : LEAD + rows]
    pad[q, LEAD + rows : LEAD + rows + 1] = pad[q, LEAD : LEAD + 1]


def fill_pad(pad, p, part, rows, step, lanes):
    planes = -(-lanes // 128)
    for start in range(0, rows, step):
        value = part(start, step)
        rng = slice(LEAD + start, LEAD + start + step)
        if lanes < 128:
            pad[p, rng, 0:lanes] = value
        else:
            for h in range(planes):
                pad[planes * p + h, rng] = value[:, 128 * h : 128 * h + 128]
    for h in range(planes):
        wrap_rows(pad, planes * p + h, rows)


def restrict_y(pad, p, rows, hi_ref, lo_ref, out_start, lanes, step=16):
    half = rows // 2
    step = min(step, half)
    planes = -(-lanes // 128)
    width = min(lanes, 128)
    for start in range(0, half, step):
        for h in range(planes):
            at = LEAD + 2 * start
            q = planes * p + h
            outer = pad[q, pl.ds(at - 1, step, stride=2), :] + pad[q, pl.ds(at + 2, step, stride=2), :]
            inner = pad[q, pl.ds(at, step, stride=2), :] + pad[q, pl.ds(at + 1, step, stride=2), :]
            value = (outer + 3.0 * inner)[:, 0:width]
            hi = value.astype(BF16)
            rng = slice(out_start + start, out_start + start + step)
            cols = slice(128 * h, 128 * h + width)
            hi_ref[rng, cols] = hi
            lo_ref[rng, cols] = (value - hi.astype(F32)).astype(BF16)


def prolong_y(pad, p, rows, wide, q):
    step = min(rows, 32)
    for start in range(0, rows, step):
        at = LEAD + start
        centre = 3.0 * pad[p, at : at + step]
        wide[q, pl.ds(2 * start, step, stride=2), :] = centre + pad[p, at - 1 : at - 1 + step]
        wide[q, pl.ds(2 * start + 1, step, stride=2), :] = centre + pad[p, at + 1 : at + 1 + step]


def y_rows(src, lead, dst, half_rows):
    for start in range(0, half_rows, 16):
        for h in range(2):
            at = lead + 2 * start
            plane = src(h)
            outer = plane[pl.ds(at - 1, 16, stride=2), :] + plane[pl.ds(at + 2, 16, stride=2), :]
            inner = plane[pl.ds(at, 16, stride=2), :] + plane[pl.ds(at + 1, 16, stride=2), :]
            dst(h, start, outer + 3.0 * inner)


def split_at(value, hi, lo, row, col):
    top = value.astype(BF16)
    rows = slice(row, row + value.shape[0])
    cols = slice(col, col + value.shape[1])
    hi[rows, cols] = top
    lo[rows, cols] = (value - top.astype(F32)).astype(BF16)


def x_rows(ybuf, c, rows, weights, hi, lo, at):
    for start in range(0, 64, 16):
        for h in range(2):
            parts = [ybuf[c, r, h, start : start + 16] for r in rows]
            ones = [p for p, w in zip(parts, weights) if w == 1]
            threes = [p for p, w in zip(parts, weights) if w == 3]
            value = sum(ones[1:], ones[0]) if ones else None
            if threes:
                heavy = 3.0 * sum(threes[1:], threes[0])
                value = heavy if value is None else value + heavy
            split_at(value, hi, lo, at + start, 128 * h)


def linear_kernel(void_hbm, slip_hbm, class_hbm, v_ref, even_ref, odd_ref, fields, class_ref, ybuf, hi, lo, wbuf, pad2, pad3, classes, sems, class_sem):
    parity = lax.axis_index("blk") % 2

    def copies(k):
        rows = pl.ds(2 * k, 2)
        y = pl.ds(LEAD, NY)
        out = []
        for h in range(2):
            z = pl.ds(128 * h, 128)
            out.append(pltpu.make_async_copy(void_hbm.at[rows, :, z], fields.at[0, rows, h, y], sems.at[k, h]))
            out.append(pltpu.make_async_copy(slip_hbm.at[:, rows, :, z], fields.at[pl.ds(1, 3), rows, h, y], sems.at[k, 2 + h]))
        return out

    class_copy = pltpu.make_async_copy(class_hbm, classes, class_sem)
    class_copy.start()
    order = (0, 7, 1, 6, 2, 5, 3, 4)
    for k in order:
        for copy in copies(k):
            copy.start()
    for c in range(4):
        for row in (0, ROWS + 1):
            for h in range(2):
                ybuf[c, row, h] = jnp.zeros((64, 128), F32)
    table = restrict_z(NZ)
    table_lo = restrict_z(128, 128, 0)
    table_hi = restrict_z(128, 128, 64)
    table3 = [restrict_z(64, 128, 32 * c) for c in range(4)]
    class_copy.wait()
    class_ref[...] = classes[...].astype(F32)

    def along_y(k):
        for copy in copies(k):
            copy.wait()
        for c in range(4):
            for r in range(2):
                row = 2 * k + r
                for h in range(2):
                    wrap_plane(fields, (c, row, h), NY)

                def put(h, start, value):
                    ybuf[c, row + 1, h, start : start + 16] = value

                y_rows(lambda h: fields.at[c, row, h], LEAD, put, 64)

    def along_x(i, at):
        base = 2 * i
        for c in range(4):
            x_rows(ybuf, c, (base, base + 1, base + 2, base + 3), (1, 3, 3, 1), hi, lo, at + 64 * c)
        out = dot2(hi[at : at + 256], lo[at : at + 256], table)
        for c in range(4):
            v_ref[c, i] = out[c * 64 : c * 64 + 64]

    def side_rows(ref, last, at):
        r0 = jnp.where(last == 1, ROWS, 1)
        r1 = jnp.where(last == 1, ROWS - 1, 2)
        r2 = jnp.where(last == 1, ROWS - 2, 3)
        for c in range(4):
            x_rows(ybuf, c, (r0,), (1,), hi, lo, at + 64 * c)
            x_rows(ybuf, c, (r0, r1, r2), (3, 3, 1), hi, lo, at + 256 + 64 * c)
        ref[0:512] = dot2(hi[at : at + 512], lo[at : at + 512], table)

    for k in order[:4]:
        along_y(k)
    for k, ready in zip(order[4:], ((0, 7), (1,), (6, 2), (3, 4, 5))):
        along_y(k)
        if k == 5:
            side_rows(odd_ref, parity, 2560)
        if k == 3:
            side_rows(even_ref, 1 - parity, 2048)
        for i in ready:
            along_x(i, 256 * i)

    table2 = restrict_z(128)
    for m in range(2):
        for c in range(4):
            fill_pad(
                pad2,
                4 * m + c,
                lambda s, t: (v_ref[c, 2 * m + 1, pl.ds(s, t)] + v_ref[c, 2 * m + 4, pl.ds(s, t)])
                + 3.0 * (v_ref[c, 2 * m + 2, pl.ds(s, t)] + v_ref[c, 2 * m + 3, pl.ds(s, t)]),
                64,
                32,
                128,
            )
            restrict_y(pad2, 4 * m + c, 64, hi, lo, 32 * (4 * m + c), 128)
    out = dot2(hi[0:256, 0:128], lo[0:256, 0:128], table2)
    for m in range(2):
        for c in range(4):
            wbuf[c, m] = out[32 * (4 * m + c) : 32 * (4 * m + c) + 32]

    def side_levels(ref, last, slot):
        n1 = jnp.where(last == 1, 6, 1)
        n2 = jnp.where(last == 1, 5, 2)
        at = 256 + 128 * slot
        for c in range(4):
            p = 8 + 4 * slot + c
            fill_pad(pad2, p, lambda s, t: 3.0 * v_ref[c, n1, pl.ds(s, t)] + v_ref[c, n2, pl.ds(s, t)], 64, 32, 128)
            restrict_y(pad2, p, 64, hi, lo, at + 32 * c, 128)
        for half in range(2):
            row = at + 64 * half
            ref[512 + 32 * half : 544 + 32 * half] = dot2(
                hi[row : row + 32, 0:128], lo[row : row + 32, 0:128], table_lo
            ) + dot2(hi[row + 32 : row + 64, 0:128], lo[row + 32 : row + 64, 0:128], table_hi)
        m1 = jnp.where(last == 1, 1, 0)
        m2 = jnp.where(last == 1, 0, 1)
        at = 512 + 64 * slot
        for c in range(4):
            p = 4 * slot + c
            fill_pad(pad3, p, lambda s, t: 3.0 * wbuf[c, m1, pl.ds(s, t)] + wbuf[c, m2, pl.ds(s, t)], 32, 32, 64)
            restrict_y(pad3, p, 32, hi, lo, at + 16 * c, 64)
        total = jnp.zeros((16, 128), F32)
        for c in range(4):
            row = at + 16 * c
            total = total + dot2(hi[row : row + 16, 0:64], lo[row : row + 16, 0:64], table3[c])
        ref[576:592] = total
        outer = jnp.where(last == 1, class_ref[1], class_ref[0])
        ref[592:608] = jnp.concatenate([outer, jnp.zeros((16, 96), F32)], axis=1)

    side_levels(even_ref, 1 - parity, 0)
    side_levels(odd_ref, parity, 1)


def wrap_plane(ref, index, rows):
    plane = ref.at[index]
    plane[LEAD - 1 : LEAD] = plane[LEAD + rows - 1 : LEAD + rows]
    plane[LEAD + rows : LEAD + rows + 1] = plane[LEAD : LEAD + 1]


def linear_call(void, slip, classes):
    hbm = pl.BlockSpec(memory_space=pltpu.HBM)
    vmem = pl.BlockSpec(memory_space=pltpu.VMEM)
    return pl.pallas_call(
        linear_kernel,
        out_shape=(
            jax.ShapeDtypeStruct((4, 8, 64, 128), F32),
            jax.ShapeDtypeStruct((608, 128), F32),
            jax.ShapeDtypeStruct((608, 128), F32),
            jax.ShapeDtypeStruct((4, ROWS, 2, NY + 16, 128), F32),
            jax.ShapeDtypeStruct((2, 16, 32), F32),
        ),
        in_specs=[hbm, hbm, hbm],
        out_specs=(vmem,) * 5,
        scratch_shapes=[
            pltpu.VMEM((4, ROWS + 2, 2, 64, 128), F32),
            pltpu.VMEM((3072, NZ), BF16),
            pltpu.VMEM((3072, NZ), BF16),
            pltpu.VMEM((4, 2, 32, 64), F32),
            pltpu.VMEM((16, 64 + 16, 128), F32),
            pltpu.VMEM((8, 32 + 16, 128), F32),
            pltpu.VMEM((2, 16, 32), jnp.int32),
            pltpu.SemaphoreType.DMA((8, 4)),
            pltpu.SemaphoreType.DMA,
        ],
        compiler_params=pltpu.CompilerParams(vmem_limit_bytes=14 << 20),
        name="linear_part",
    )(void, slip, classes)


def drag_kernel(fields, class_ref, scale_ref, g_ref, filt_ref, edge_ref, kappa, ybuf, hi, lo):
    pairs = ROWS // 2
    for c in range(3):
        for row in (0, ROWS + 1):
            for h in range(2):
                ybuf[c, row, h] = jnp.zeros((64, 128), F32)
    for b in range(2):
        kappa[b] = class_factor(scale_ref, spread(class_ref[b], 16, NZ))
    table = restrict_z(NZ)

    def drag_rows(k):
        block = k // 4
        for r in range(2):
            x = 2 * k + r
            for y in range(16):
                rows = slice(LEAD + 8 * y, LEAD + 8 * y + 8)
                for h in range(2):
                    factor = jnp.broadcast_to(kappa[block, y : y + 1, 128 * h : 128 * h + 128], (8, 128))
                    g = drag(*(fields[c, x, h, rows] for c in range(4)), factor)
                    for c in range(3):
                        g_ref[c, x, h, rows] = g[c]
            for c in range(3):
                for h in range(2):
                    wrap_plane(g_ref, (c, x, h), NY)

    def along_y(k):
        for c in range(3):
            for r in range(2):
                row = 2 * k + r

                def put(h, start, value):
                    ybuf[c, row + 1, h, start : start + 16] = value

                y_rows(lambda h: g_ref.at[c, row, h], LEAD, put, 64)

    def along_x(i, at):
        base = 2 * i
        for c in range(3):
            x_rows(ybuf, c, (base, base + 1, base + 2, base + 3), (1, 3, 3, 1), hi, lo, at + 64 * c)
        out = dot2(hi[at : at + 192], lo[at : at + 192], table)
        for c in range(3):
            filt_ref[c, i] = out[c * 64 : c * 64 + 64]

    drag_rows(0)
    drag_rows(1)
    along_y(0)

    def body(i, carry):
        drag_rows(i + 2)
        along_y(i + 1)
        along_x(i, 0)
        return carry

    lax.fori_loop(0, pairs - 2, body, 0)
    along_y(pairs - 1)
    along_x(pairs - 2, 0)
    along_x(pairs - 1, 192)
    for e, row in enumerate((1, ROWS)):
        at = 384 + 192 * e
        for c in range(3):
            x_rows(ybuf, c, (row,), (1,), hi, lo, at + 64 * c)
        out = dot2(hi[at : at + 192], lo[at : at + 192], table)
        for c in range(3):
            edge_ref[e, c] = out[c * 64 : c * 64 + 64]


def drag_call(fields, classes, scale):
    vmem = pl.BlockSpec(memory_space=pltpu.VMEM)
    return pl.pallas_call(
        drag_kernel,
        out_shape=(
            jax.ShapeDtypeStruct((3, ROWS, 2, NY + 16, 128), F32),
            jax.ShapeDtypeStruct((3, 8, 64, 128), F32),
            jax.ShapeDtypeStruct((2, 3, 64, 128), F32),
        ),
        in_specs=[vmem, vmem, pl.BlockSpec(memory_space=pltpu.SMEM)],
        out_specs=(vmem,) * 3,
        scratch_shapes=[
            pltpu.VMEM((2, 16, NZ), F32),
            pltpu.VMEM((3, ROWS + 2, 2, 64, 128), F32),
            pltpu.VMEM((768, NZ), BF16),
            pltpu.VMEM((768, NZ), BF16),
        ],
        compiler_params=pltpu.CompilerParams(vmem_limit_bytes=10 << 20),
        cost_estimate=pl.CostEstimate(flops=60_000_000, bytes_accessed=16_000_000, transcendentals=1_500_000),
        name="drag_part",
    )(fields, classes, scale)


def x_prolong(planes, count):
    for f in range(-1, 2 * count + 1):
        centre = (f >> 1) + 1
        beside = centre + (1 if f & 1 else -1)
        yield f + 1, 3.0 * planes(centre) + planes(beside)


def plain_prolong_z(length):
    coarse = iota((length, 2 * length), 0)
    fine = iota((length, 2 * length), 1)
    centre = lax.shift_right_logical(fine, 1)
    neighbour = jnp.clip(centre - 1 + 2 * (fine & 1), 0, length - 1)
    return (jnp.where(coarse == centre, 3.0, 0.0) + jnp.where(coarse == neighbour, 1.0, 0.0)).astype(BF16)


def make_table(table_ref):
    first = plain_prolong_z(128)
    second = jnp.dot(plain_prolong_z(64), first, preferred_element_type=F32)
    third = jnp.dot(plain_prolong_z(32), plain_prolong_z(64), preferred_element_type=F32)
    third = jnp.dot(third.astype(BF16), first, preferred_element_type=F32)
    table_ref[0:128] = (first.astype(F32) * (1.0 / 64.0)).astype(BF16)
    table_ref[128:192] = (second * (1.0 / 64.0**2)).astype(BF16)
    table_ref[192:224] = (third * (1.0 / 64.0**3)).astype(BF16)
    table_ref[224:256] = jnp.zeros((32, NZ), BF16)


def put_wide(pad, q, part, wide, to):
    pad[q, LEAD : LEAD + 64] = part
    wrap_rows(pad, q, 64)
    prolong_y(pad, q, 64, wide, to)


def x_part(plane, c, i, count):
    def part(start, step):
        rows = pl.ds(start, step)
        if i == -1:
            return 3.0 * plane(c, -1)[rows] + plane(c, 0)[rows]
        if i == count:
            return plane(c, 2 * count - 1)[rows] + 3.0 * plane(c, 2 * count)[rows]
        return (plane(c, 2 * i - 1)[rows] + plane(c, 2 * i + 2)[rows]) + 3.0 * (
            plane(c, 2 * i)[rows] + plane(c, 2 * i + 1)[rows]
        )

    return part


def total(values):
    return jnp.sum(values, axis=0, keepdims=True)


def inner_kernel(v_in, filt_ref, class_ref, scale_ref, g1_ref, w_ref, g2_ref, wide_ref, table_ref, kap1_ref, kap2_ref, sums_ref, pad, pad1, hi, lo):
    make_table(table_ref)
    for b in range(2):
        kap1_ref[b] = class_factor(scale_ref, spread(class_ref[b], 64, 128))
        kap2_ref[b] = class_factor(scale_ref, spread(class_ref[b], 32, 64))
    numerator = jnp.zeros((64, 128), F32)
    denominator = jnp.zeros((64, 128), F32)
    for i in range(1, 7):
        slips = v_in[1, i], v_in[2, i], v_in[3, i]
        g = drag(v_in[0, i], *slips, kap1_ref[i // 4])
        for c in range(3):
            g1_ref[c, i - 1] = g[c]
            numerator += filt_ref[c, i] * slips[c]
            denominator += g[c] * slips[c]
            put_wide(pad1, 6 * c + i - 1, g[c], wide_ref, 6 * c + i - 1)
    sums_ref[0:1] = total(numerator)
    sums_ref[1:2] = total(denominator)
    n = 0
    for count, plane in ((4, lambda c, i: v_in.at[c, i]), (3, lambda c, i: g1_ref.at[c, i - 1])):
        for i in (1, 2):
            for c in range(count):
                fill_pad(pad, n, x_part(plane, c, i, 4), 64, 32, 128)
                restrict_y(pad, n, 64, hi, lo, 32 * n, 128)
                n += 1
    out = dot2(hi[...], lo[...], restrict_z(128))
    numerator = jnp.zeros((32, 64), F32)
    denominator = jnp.zeros((32, 64), F32)
    for i in (1, 2):
        channels = [out[32 * (4 * (i - 1) + c) : 32 * (4 * (i - 1) + c) + 32] for c in range(4)]
        g = drag(*channels, kap2_ref[i // 2])
        for c in range(4):
            w_ref[c, i - 1] = channels[c]
        for c in range(3):
            g2_ref[c, i - 1] = g[c]
            at = 32 * (8 + 3 * (i - 1) + c)
            numerator += out[at : at + 32] * channels[c + 1]
            denominator += g[c] * channels[c + 1]
    blank = jnp.zeros((1, 64), F32)
    sums_ref[2:3] = jnp.concatenate([total(numerator), blank], axis=1)
    sums_ref[3:4] = jnp.concatenate([total(denominator), blank], axis=1)
    sums_ref[4:8] = jnp.zeros((4, 128), F32)


def inner_call(v_part, filt, classes, scale):
    vmem = pl.BlockSpec(memory_space=pltpu.VMEM)
    return pl.pallas_call(
        inner_kernel,
        out_shape=(
            jax.ShapeDtypeStruct((3, 6, 64, 128), F32),
            jax.ShapeDtypeStruct((4, 2, 32, 64), F32),
            jax.ShapeDtypeStruct((3, 2, 32, 64), F32),
            jax.ShapeDtypeStruct((18, NY, 128), F32),
            jax.ShapeDtypeStruct((256, NZ), BF16),
            jax.ShapeDtypeStruct((2, 64, 128), F32),
            jax.ShapeDtypeStruct((2, 32, 64), F32),
            jax.ShapeDtypeStruct((8, 128), F32),
        ),
        in_specs=[vmem] * 3 + [pl.BlockSpec(memory_space=pltpu.SMEM)],
        out_specs=(vmem,) * 8,
        scratch_shapes=[
            pltpu.VMEM((14, 64 + 16, 128), F32),
            pltpu.VMEM((18, 64 + 16, 128), F32),
            pltpu.VMEM((14 * 32, 128), BF16),
            pltpu.VMEM((14 * 32, 128), BF16),
        ],
        compiler_params=pltpu.CompilerParams(vmem_limit_bytes=8 << 20),
        cost_estimate=pl.CostEstimate(flops=20_000_000, bytes_accessed=4_000_000, transcendentals=300_000),
        name="inner_levels",
    )(v_part, filt, classes, scale)


def levels_kernel(
    v_in, even_own, odd_own, even_in, odd_in, filt_ref, edge_ref, class_ref, scale_ref,
    g1_in, w_in, g2_in, kap1_ref, kap2_ref, part_ref,
    wide_ref, sums_ref,
    v, g1, w, g2, g3, pad, padw, hi, lo, pad3, up3, pad2, up2, pad1,
):
    is_even = lax.axis_index("blk") % 2 == 0

    def left(rows):
        return jnp.where(is_even, odd_in[rows], even_in[rows])

    def right(rows):
        return jnp.where(is_even, even_in[rows], odd_in[rows])

    def own_first(rows):
        return jnp.where(is_even, odd_own[rows], even_own[rows])

    def own_last(rows):
        return jnp.where(is_even, even_own[rows], odd_own[rows])

    slot1 = {-1: 0, 0: 1, 7: 2, 8: 3}
    slot2 = {-1: 0, 0: 1, 3: 2, 4: 3}

    def plane_v(c, i):
        return v.at[c, slot1[i]] if i in slot1 else v_in.at[c, i]

    def plane_g1(c, i):
        return g1.at[c, slot1[i]] if i in slot1 else g1_in.at[c, i - 1]

    def plane_w(c, i):
        return w.at[c, slot2[i]] if i in slot2 else w_in.at[c, i - 1]

    def plane_g2(c, i):
        return g2.at[c, slot2[i]] if i in slot2 else g2_in.at[c, i - 1]

    for c in range(4):
        outer = slice(64 * c, 64 * c + 64)
        combined = slice(256 + 64 * c, 256 + 64 * c + 64)
        v[c, 0] = left(combined) + own_first(outer)
        v[c, 1] = v_in[c, 0] + left(outer)
        v[c, 2] = v_in[c, 7] + right(outer)
        v[c, 3] = right(combined) + own_last(outer)
    beyond = left(slice(592, 608))[:, 0:32], right(slice(592, 608))[:, 0:32]
    factors = {
        -1: class_factor(scale_ref, spread(beyond[0], 64, 128)),
        0: kap1_ref[0],
        7: kap1_ref[1],
        8: class_factor(scale_ref, spread(beyond[1], 64, 128)),
    }
    numerator = jnp.zeros((64, 128), F32)
    denominator = jnp.zeros((64, 128), F32)
    for i, n in slot1.items():
        slips = v[1, n], v[2, n], v[3, n]
        g = drag(v[0, n], *slips, factors[i])
        for c in range(3):
            g1[c, n] = g[c]
            if i == -1:
                numerator += edge_ref[0, c] * slips[c]
            elif i == 8:
                numerator += edge_ref[1, c] * slips[c]
            else:
                numerator += filt_ref[c, i] * slips[c]
                denominator += g[c] * slips[c]
    sums = [total(numerator) + part_ref[0:1], total(denominator) + part_ref[1:2]]

    n = 0
    for count, plane, rows in ((4, plane_v, (-1, 0, 3, 4)), (3, plane_g1, (0, 3))):
        for i in rows:
            for c in range(count):
                fill_pad(pad, n, x_part(plane, c, i, 4), 64, 32, 128)
                restrict_y(pad, n, 64, hi, lo, 32 * n, 128)
                n += 1
    out = dot2(hi[0 : 32 * n, 0:128], lo[0 : 32 * n, 0:128], restrict_z(128))
    factors = {
        -1: class_factor(scale_ref, spread(beyond[0], 32, 64)),
        0: kap2_ref[0],
        3: kap2_ref[1],
        4: class_factor(scale_ref, spread(beyond[1], 32, 64)),
    }
    numerator = jnp.zeros((32, 64), F32)
    denominator = jnp.zeros((32, 64), F32)
    for i, n in slot2.items():
        channels = []
        for c in range(4):
            value = out[32 * (4 * n + c) : 32 * (4 * n + c) + 32]
            if i in (-1, 4):
                rows = slice(512 + 32 * (c // 2), 544 + 32 * (c // 2))
                more = left(rows) if i == -1 else right(rows)
                if c % 2:
                    more = pltpu.roll(more, 64, 1)
                value = value + more[:, 0:64]
            w[c, n] = value
            channels.append(value)
        g = drag(*channels, factors[i])
        for c in range(3):
            g2[c, n] = g[c]
            if i in (0, 3):
                at = 32 * (16 + 3 * (n - 1) + c)
                numerator += out[at : at + 32] * channels[c + 1]
                denominator += g[c] * channels[c + 1]
    sums += [total(numerator) + part_ref[2:3, 0:64], total(denominator) + part_ref[3:4, 0:64]]

    n = 0
    for count, plane, rows in ((4, plane_w, (-1, 0, 1, 2)), (3, plane_g2, (0, 1))):
        for i in rows:
            for c in range(count):
                fill_pad(padw, n, x_part(plane, c, i, 2), 32, 32, 64)
                restrict_y(padw, n, 32, hi, lo, 16 * n, 64)
                n += 1
    out = dot2(hi[0 : 16 * n, 0:64], lo[0 : 16 * n, 0:64], restrict_z(64))
    numerator = jnp.zeros((16, 32), F32)
    denominator = jnp.zeros((16, 32), F32)
    blocks = [beyond[0], class_ref[0], class_ref[1], beyond[1]]
    for i in range(4):
        channels = []
        for c in range(4):
            value = out[16 * (4 * i + c) : 16 * (4 * i + c) + 16]
            if i == 0 or i == 3:
                more = left(slice(576, 592)) if i == 0 else right(slice(576, 592))
                if c:
                    more = pltpu.roll(more, 128 - 32 * c, 1)
                value = value + more[:, 0:32]
            channels.append(value)
        g = drag(*channels, class_factor(scale_ref, blocks[i]))
        for c in range(3):
            g3[c, i] = g[c]
            if 1 <= i <= 2:
                at = 16 * (16 + 3 * (i - 1) + c)
                numerator += out[at : at + 16] * channels[c + 1]
                denominator += g[c] * channels[c + 1]
    sums += [total(numerator), total(denominator)]
    ones = jnp.ones((1, 32), F32)
    packed = [sums[0], sums[1]] + [jnp.concatenate([sums[2 + k], sums[4 + k], ones], axis=1) for k in range(2)]
    tile = jnp.concatenate(packed, axis=0)
    for d in range(16):
        sums_ref[d] = tile

    for c in range(3):
        for e in range(4):
            p = 4 * c + e
            pad3[p, LEAD : LEAD + 16, 0:32] = g3[c, e]
            wrap_rows(pad3, p, 16)
            prolong_y(pad3, p, 16, up3, p)
        for f, value in x_prolong(lambda e: up3[4 * c + e], 2):
            p = 6 * c + f
            pad2[p, LEAD : LEAD + 32] = jnp.concatenate(
                [plane_g2(c, f - 1)[...], value[:, 0:32], jnp.zeros((32, 32), F32)], axis=1
            )
            wrap_rows(pad2, p, 32)
            prolong_y(pad2, p, 32, up2, p)
        for f, value in x_prolong(lambda e: up2[6 * c + e], 4):
            put_wide(pad1, 10 * c + f, value, wide_ref, 10 * c + f)
        for n in slot1.values():
            put_wide(pad1, 30 + 4 * c + n, g1[c, n], wide_ref, 30 + 4 * c + n)


def levels_call(v_part, even_own, odd_own, even_in, odd_in, filt, edge, classes, scale, g1, w, g2, kap1, kap2, part):
    vmem = pl.BlockSpec(memory_space=pltpu.VMEM)
    return pl.pallas_call(
        levels_kernel,
        out_shape=(
            jax.ShapeDtypeStruct((42, NY, 128), F32),
            jax.ShapeDtypeStruct((16, 4, 128), F32),
        ),
        in_specs=[vmem] * 8 + [pl.BlockSpec(memory_space=pltpu.SMEM)] + [vmem] * 6,
        out_specs=(vmem,) * 2,
        scratch_shapes=[
            pltpu.VMEM((4, 4, 64, 128), F32),
            pltpu.VMEM((3, 4, 64, 128), F32),
            pltpu.VMEM((4, 4, 32, 64), F32),
            pltpu.VMEM((3, 4, 32, 64), F32),
            pltpu.VMEM((3, 4, 16, 32), F32),
            pltpu.VMEM((22, 64 + 16, 128), F32),
            pltpu.VMEM((22, 32 + 16, 128), F32),
            pltpu.VMEM((22 * 32, 128), BF16),
            pltpu.VMEM((22 * 32, 128), BF16),
            pltpu.VMEM((12, 16 + 16, 128), F32),
            pltpu.VMEM((12, 32, 128), F32),
            pltpu.VMEM((18, 32 + 16, 128), F32),
            pltpu.VMEM((18, 64, 128), F32),
            pltpu.VMEM((42, 64 + 16, 128), F32),
        ],
        compiler_params=pltpu.CompilerParams(vmem_limit_bytes=12 << 20),
        name="small_levels",
    )(v_part, even_own, odd_own, even_in, odd_in, filt, edge, classes, scale, g1, w, g2, kap1, kap2, part)


def final_kernel(sums_ref, inner_ref, wide_ref, table_ref, g0_ref, out_hbm, stage, hi, lo, fine, sems):
    added = jnp.sum(sums_ref[...], axis=0)
    ratios = [added[2 * h : 2 * h + 1] / added[2 * h + 1 : 2 * h + 2] - 1.0 for h in range(2)]

    def wide(c, e, h):
        if h:
            return wide_ref.at[10 * c + e]
        if 2 <= e <= 7:
            return inner_ref.at[6 * c + e - 2]
        return wide_ref.at[30 + 4 * c + {0: 0, 1: 1, 8: 2, 9: 3}[e]]

    def make_fine(e):
        slot = e % 2
        for c in range(3):
            for h in range(2):
                for start in range(0, NY, 16):
                    value = wide(c, e, h)[start : start + 16] * ratios[h]
                    split_at(value, hi.at[slot], lo.at[slot], NY * c + start, 128 * h)
        values = dot2(hi[slot], lo[slot], table_ref[...])
        for c in range(3):
            fine[e, c] = values[NY * c : NY * c + NY]

    def out_copy(row):
        return pltpu.make_async_copy(stage.at[:, row], out_hbm.at[:, row], sems.at[row])

    def make_rows(step, both):
        for c in range(3):
            for h in range(2):
                cols = slice(128 * h, 128 * h + 128)
                for start in range(0, NY, 16):
                    rows = slice(start, start + 16)
                    lead = slice(LEAD + start, LEAD + start + 16)
                    centre = 3.0 * fine[step + 1, c, rows, cols]
                    for half in both:
                        beside = fine[step + 2 * half, c, rows, cols]
                        stage[c, 2 * step + half, rows, cols] = g0_ref[c, 2 * step + half, h, lead] + (centre + beside)
        for half in both:
            out_copy(2 * step + half).start()

    make_fine(0)
    make_fine(1)
    make_fine(2)
    make_rows(0, (0,))
    make_fine(3)
    make_rows(0, (1,))
    for step in range(1, 8):
        if step < 7:
            make_fine(step + 3)
        make_rows(step, (0, 1))
    for row in range(ROWS):
        out_copy(row).wait()


def final_call(sums, inner, wide, table, g0):
    vmem = pl.BlockSpec(memory_space=pltpu.VMEM)
    return pl.pallas_call(
        final_kernel,
        out_shape=jax.ShapeDtypeStruct((3, ROWS, NY, NZ), F32),
        in_specs=[vmem] * 5,
        out_specs=pl.BlockSpec(memory_space=pltpu.HBM),
        scratch_shapes=[
            pltpu.VMEM((3, ROWS, NY, NZ), F32),
            pltpu.VMEM((2, 3 * NY, NZ), BF16),
            pltpu.VMEM((2, 3 * NY, NZ), BF16),
            pltpu.VMEM((10, 3, NY, NZ), F32),
            pltpu.SemaphoreType.DMA((ROWS,)),
        ],
        compiler_params=pltpu.CompilerParams(vmem_limit_bytes=16 << 20),
        name="final_part",
    )(sums, inner, wide, table, g0)


def shards(void_fraction, slip_velocity, size_class, class_scale):
    count = lax.axis_size("blk")
    even_pairs = [(i, i ^ 1) for i in range(count)]
    odd_pairs = [(i, (i + 1) % count if i % 2 else (i - 1) % count) for i in range(count)]
    void_fraction, slip_velocity, size_class = (
        pltpu.with_memory_space_constraint(x, pltpu.HBM) for x in (void_fraction, slip_velocity, size_class)
    )
    v_part, even_own, odd_own, fields, classes = linear_call(void_fraction, slip_velocity, size_class)
    odd_in = lax.ppermute(odd_own, "blk", odd_pairs)
    even_in = lax.ppermute(even_own, "blk", even_pairs)
    g0, filt, edge = drag_call(fields, classes, class_scale)
    g1, w, g2, inner, table, kap1, kap2, part = inner_call(v_part, filt, classes, class_scale)
    wide, sums = levels_call(
        v_part, even_own, odd_own, even_in, odd_in, filt, edge, classes, class_scale, g1, w, g2, kap1, kap2, part
    )
    sums = lax.all_to_all(sums, "blk", 0, 0)
    return final_call(sums, inner, wide, table, g0)


def solution(mesh):
    return jax.shard_map(
        shards,
        mesh=mesh,
        in_specs=(P("blk", None, "grp"), P(None, "blk", None, "grp"), P("blk", None, "grp"), P()),
        out_specs=P(None, "blk", None, "grp"),
        check_vma=False,
    )
```
